128 devices in a mesh: dp: 8 (over z, x_hi), mp: 16 (over y, x_lo, core).
Axes of the slice: x: 4 (x_hi: 2, x_lo: 2; x = x_hi * 2 + x_lo), y: 4, z: 4, core: 2. Of those that a mesh axis runs over, the one named last changes fastest.
Arguments:
- tokens: bfloat16 [16384, 2048], P(('dp', 'mp')), may hold values from -6 to 6
- attn_gain: float32 [2048], replicated, may hold values from 0.25 to 1.75
- mlp_gain: float32 [2048], replicated, may hold values from 0.25 to 1.75
- query_weight: bfloat16 [2048, 2048], replicated, as said below
- keyval_weight: bfloat16 [2048, 1024], replicated, as said below
- output_weight: bfloat16 [2048, 2048], replicated, may hold values from -0.125 to 0.125
- gate_rows: float32 [2048, 8192], P(('dp', 'mp')), may hold values from -0.125 to 0.125
- up_rows: float32 [2048, 8192], P(('dp', 'mp')), may hold values from -0.125 to 0.125
- down_rows: float32 [8192, 2048], P(('dp', 'mp')), may hold values from -0.0625 to 0.0625
- lengths: int32 [8, 1], P('dp'), may hold values from 1024 to 2048
- valid: int32 [16384], P(('dp', 'mp')), may hold values 0 or 1
- page_table: int32 [1024, 1], P(('dp', 'mp')), may hold values from 0 to 7; in each aligned block of 8 rows (0 to 7, 8 to 15, ...) at most 2 rows name the same one
Outputs:
- layer_out: bfloat16 [16384, 2048], P(('dp', 'mp'))
- page_cache: bfloat16 [8, 16, 8, 2, 16, 1024], P('dp', 'mp')
The draws below stay inside these ranges and needn't reach their ends.
Inputs may be any that keep to these rules, and one draw needn't show every extreme that they name: `page_table`: of the 8 pages of one device at most 2 name the same holder; in every draw some device sends 2 pages to one holder. `query_weight`: entries are independent, of mean zero. `keyval_weight`: entries are independent, of mean zero.
All inputs are finite; a program needn't handle non-finite values. No bound on the sum of `valid` on one device may be relied on, other than what follows from the above.
Results may differ from the reference program's by a relative error of at most 0.02.
The reference program's roundings to bfloat16 on the way count: a program that leaves them out, or rounds other values in their place, can miss the bound.
Values may be sent and summed in bfloat16 or wider, within the bound.
A program may use at most 128 MiB of HBM per device.

```python
import math
import jax
import jax.numpy as jnp
import numpy as np
from jax import lax

D = 2048
QH = 32
KVH = 8
HD = 64
FF = 8192
TOK_DEV = 128
PAGE = 16
PAGE_MOST = 2
PROMPTS_GRP = 1
TOK_GRP = 2048
TOKENS = 16384
PAGES = 1024
N_DP = 8
N_MP = 16


def draw_query_weight(key, part):
    base = jax.random.normal(key, (D, QH * HD), jnp.float32) * D ** (-0.5)
    return base.astype(jnp.bfloat16)


def draw_keyval_weight(key, part):
    base = jax.random.normal(key, (D, 2 * KVH * HD), jnp.float32) * D ** (-0.5)
    return base.astype(jnp.bfloat16)


def touch_ends(values, own_key, smallest, largest):
    spot = [jax.random.randint(jax.random.fold_in(own_key, axis), (), 0, length) for axis, length in enumerate(values.shape)]
    main_axis = values.shape.index(max(values.shape))
    next_to = spot[:main_axis] + [(spot[main_axis] + 1) % values.shape[main_axis]] + spot[main_axis + 1:]
    return values.at[tuple(spot)].set(smallest).at[tuple(next_to)].set(largest)


def level_of(stream_key, dims, cuts, least, largest):
    def one(axis_at, parts):
        draws = jax.random.uniform(jax.random.fold_in(jax.random.fold_in(stream_key, 6), axis_at), (parts,), jnp.float32, least / len(cuts), largest / len(cuts))
        return jnp.repeat(jnp.exp(draws), dims[axis_at] // parts).reshape((-1,) + (1,) * (len(dims) - axis_at - 1))

    loudness = one(*cuts[0])
    for cut in cuts[1:]:
        loudness = loudness * one(*cut)
    return loudness


def shared_out(key, own, number, rows, count, top, bound, slope):
    sequence = jax.random.permutation(key, count)
    crowded, usual = portions_of(count, rows * top, bound, slope, True), portions_of(count, rows * top, bound, slope, False)
    places = jnp.arange(count)

    def named(sizes, rotation):
        used = int((sizes > 0).sum())
        fixed = max(1, used // 4)
        shifted = fixed + (places - fixed + rotation * (used - fixed)) % max(1, count - fixed)
        return jnp.zeros((count,), jnp.int32).at[sequence[jnp.where(places < fixed, places, shifted)]].set(jnp.asarray(sizes, jnp.int32))

    sizes = jnp.where(number % 4 == 0, named(crowded, number // 4), named(usual, number - number // 4 - 1))
    mixed = jax.random.permutation(jax.random.fold_in(own, 3), count)
    source_of, taker = mixed[0:count // 2 * 2:2], mixed[1:count // 2 * 2:2]
    margin = jnp.minimum(sizes[source_of] - 1, bound - sizes[taker]) // 2
    margin = jnp.where((source_of == sequence[0]) | (taker == sequence[0]) | (sizes[taker] == 0), 0, jnp.maximum(margin, 0))
    shifted = jax.random.randint(jax.random.fold_in(own, 4), (count // 2,), 0, 1 << 20) % (margin + 1)
    sizes = sizes.at[source_of].add(-shifted).at[taker].add(shifted)
    labels = jnp.searchsorted(jnp.cumsum(sizes), jnp.arange(rows * top), side="right").astype(jnp.int32)
    table = labels.reshape(top, rows).T
    table = table[jax.random.permutation(jax.random.fold_in(own, 1), rows)]
    rotation = jax.random.randint(jax.random.fold_in(own, 2), (rows, 1), 0, top)
    return jnp.take_along_axis(table, (jnp.arange(top)[None, :] + rotation) % top, axis=1)


def portions_of(count, total, reach, lean, full):
    loads = [(1 << 20) // math.isqrt(standing ** lean) + 1 for standing in range(1, count + 1)]
    largest = reach if full else min(reach, max(-(-total // count), total * loads[0] // sum(loads)))
    least = 1 if total - largest >= count - 1 else 0
    given, rest = [largest] + [least] * (count - 1), total - largest - least * (count - 1)
    while rest > 0:
        free = [i for i in range(1, count) if given[i] < largest] or [i for i in range(1, count) if given[i] < reach]
        whole, left = sum([loads[i] for i in free]), rest
        for i in free:
            more = min(reach - given[i], max(1, left * loads[i] // whole), rest)
            given[i] = given[i] + more
            rest = rest - more
    return np.array(given)


def normal_values(rng, dims, spread, most, shards=(), held_as=jnp.bfloat16):
    level = level_of(rng, dims, shards, -0.22, 0.18) if shards else 1.0
    drawn = jax.random.normal(rng, dims, jnp.float32) * spread * level
    return jnp.minimum(jnp.maximum(drawn, -most), most).astype(held_as)


def setup_inputs(seed: int = 0) -> dict:
    streams_of = jax.random.split(jax.random.key(seed), 13)
    tokens = normal_values(streams_of[0], (TOKENS, D), 1.0, 6.0, ((0, 128),))
    attn_gain = jnp.clip(1.0 + 0.15 * jax.random.normal(streams_of[1], (D,), jnp.float32), 0.25, 1.75)
    mlp_gain = jnp.clip(1.0 + 0.15 * jax.random.normal(streams_of[2], (D,), jnp.float32), 0.25, 1.75)
    query_weight = draw_query_weight(jax.random.fold_in(streams_of[12], 71), 0)
    keyval_weight = draw_keyval_weight(jax.random.fold_in(streams_of[12], 71), 0)
    output_weight = normal_values(streams_of[5], (QH * HD, D), (QH * HD) ** -0.5, 0.125)
    gate_rows = normal_values(streams_of[6], (D, FF), D ** -0.5, 0.125, ((0, 128),), jnp.float32)
    up_rows = normal_values(streams_of[7], (D, FF), D ** -0.5, 0.125, ((0, 128),), jnp.float32)
    down_rows = normal_values(streams_of[8], (FF, D), FF ** -0.5, 0.0625, ((0, 128),), jnp.float32)
    lengths = touch_ends(jax.random.randint(streams_of[9], (N_DP, PROMPTS_GRP), TOK_GRP // 2, TOK_GRP + 1), jax.random.fold_in(streams_of[9], 1), TOK_GRP // 2, TOK_GRP).astype(jnp.int32)
    valid = touch_ends((jax.random.randint(streams_of[10], (TOKENS,), 0, 8) < 7).astype(jnp.int32), jax.random.fold_in(streams_of[10], 1), 0, 1)
    page_table_keys = jax.random.split(jax.random.fold_in(streams_of[11], 1), PAGES // (TOK_DEV // PAGE))
    page_table_turns = jax.random.permutation(jax.random.fold_in(streams_of[11], 3), PAGES // (TOK_DEV // PAGE))
    page_table = jax.vmap(lambda own, number: shared_out(jax.random.fold_in(streams_of[11], 2), own, number, TOK_DEV // PAGE, N_DP, 1, PAGE_MOST, 2))(page_table_keys, page_table_turns).reshape((PAGES, 1))
    return dict(tokens=tokens, attn_gain=attn_gain, mlp_gain=mlp_gain, query_weight=query_weight, keyval_weight=keyval_weight, output_weight=output_weight, gate_rows=gate_rows, up_rows=up_rows, down_rows=down_rows, lengths=lengths, valid=valid, page_table=page_table)


rope_base = 500000.0

def rms_scale(values, gain):
    mean_square = lax.optimization_barrier(jnp.mean(values * values, axis=-1, keepdims=True))
    return values * lax.rsqrt(mean_square + 1e-05) * gain

def prompt_ids(lens, rows):
    ends = jnp.cumsum(lens).astype(jnp.int32)
    starts = ends - lens
    segment = lax.optimization_barrier(jnp.sum((rows[:, None] >= ends[None, :]).astype(jnp.int32), axis=1)).astype(jnp.int32)
    prompt_range = jnp.arange(lens.shape[0], dtype=jnp.int32)
    first = lax.optimization_barrier(jnp.sum(jnp.where(segment[:, None] == prompt_range[None, :], starts[None, :], 0), axis=1))
    return (segment, (rows - first).astype(jnp.int32))

def rotate(heads, position):
    half = heads.shape[-1] // 2
    expo = jnp.arange(half, dtype=jnp.float32) * (2.0 / heads.shape[-1])
    inverse = jnp.exp(-expo * jnp.log(jnp.float32(rope_base)))
    angle = position.astype(jnp.float32)[:, None] * inverse[None, :]
    cosine = jnp.cos(angle)[:, None, :]
    sine = jnp.sin(angle)[:, None, :]
    first_half = heads[..., :half]
    second_half = heads[..., half:]
    return jnp.concatenate([first_half * cosine - second_half * sine, second_half * cosine + first_half * sine], axis=-1)

def reference(tokens, attn_gain, mlp_gain, query_weight, keyval_weight, output_weight, gate_rows, up_rows, down_rows, lengths, valid, page_table):
    gate_server = gate_rows.astype(jnp.bfloat16)
    up_server = up_rows.astype(jnp.bfloat16)
    down_server = down_rows.astype(jnp.bfloat16)
    group_size = 4
    unit_block = FF // N_MP

    def group_layer(inputs):
        block, lens, flags = inputs
        rows = jnp.arange(TOK_GRP, dtype=jnp.int32)
        segment, position = prompt_ids(lens, rows)
        block_f = block.astype(jnp.float32)
        normed = rms_scale(block_f, attn_gain).astype(jnp.bfloat16)
        queries = jnp.dot(normed, query_weight, preferred_element_type=jnp.float32).reshape(TOK_GRP, QH, HD)
        queries = rotate(queries, position).astype(jnp.bfloat16)
        keyval = jnp.dot(normed, keyval_weight, preferred_element_type=jnp.float32)
        keys = rotate(keyval[:, :KVH * HD].reshape(TOK_GRP, KVH, HD), position).astype(jnp.bfloat16)
        values = keyval[:, KVH * HD:].reshape(TOK_GRP, KVH, HD).astype(jnp.bfloat16)
        allowed = (segment[:, None] == segment[None, :]) & (rows[None, :] <= rows[:, None]) & ((flags[None, :] == 1) | (rows[None, :] == rows[:, None]))

        def head_group(index):
            query_part = lax.dynamic_slice_in_dim(queries, index * group_size, group_size, 1).astype(jnp.float32)
            key_part = lax.dynamic_index_in_dim(keys, index, 1, keepdims=False).astype(jnp.float32)
            value_part = lax.dynamic_index_in_dim(values, index, 1, keepdims=False).astype(jnp.float32)
            scores = jnp.einsum('thd,sd->hts', query_part, key_part) * 0.125
            scores = jnp.where(allowed[None], scores, jnp.float32(-1e+30))
            top = lax.optimization_barrier(jnp.max(scores, axis=-1, keepdims=True))
            expd = jnp.exp(scores - top)
            weights = (expd / lax.optimization_barrier(jnp.sum(expd, axis=-1, keepdims=True))).astype(jnp.bfloat16)
            return jnp.einsum('hts,sd->thd', weights.astype(jnp.float32), value_part).astype(jnp.bfloat16)
        attended = lax.map(head_group, jnp.arange(KVH, dtype=jnp.int32))
        attended = jnp.transpose(attended, (1, 0, 2, 3)).reshape(TOK_GRP, QH * HD)
        hidden_state = (block_f + jnp.dot(attended, output_weight, preferred_element_type=jnp.float32)).astype(jnp.bfloat16)
        hidden_f = hidden_state.astype(jnp.float32)
        mlp_in = rms_scale(hidden_f, mlp_gain).astype(jnp.bfloat16)
        gate = jnp.dot(mlp_in, gate_server, preferred_element_type=jnp.float32)
        upper = jnp.dot(mlp_in, up_server, preferred_element_type=jnp.float32)
        activated = (jax.nn.silu(gate) * upper).astype(jnp.bfloat16)

        def add_partial(index, total):
            start = (index * unit_block).astype(jnp.int32)
            act_part = lax.dynamic_slice_in_dim(activated, start, unit_block, 1)
            down_part = lax.dynamic_slice_in_dim(down_server, start, unit_block, 0)
            partial_value = jnp.dot(act_part, down_part, preferred_element_type=jnp.float32).astype(jnp.bfloat16)
            return total + partial_value.astype(jnp.float32)
        summed = lax.fori_loop(0, N_MP, add_partial, jnp.zeros((TOK_GRP, D), jnp.float32))
        result = (hidden_f + summed).astype(jnp.bfloat16)
        cache_rows = jnp.concatenate([keys.reshape(TOK_GRP, KVH * HD), values.reshape(TOK_GRP, KVH * HD)], axis=1)
        return (result, cache_rows)
    outputs, cache_rows = lax.map(group_layer, (tokens.reshape(N_DP, TOK_GRP, D), lengths, valid.reshape(N_DP, TOK_GRP)))
    layer_out = outputs.reshape(TOKENS, D)
    pages_dev = TOK_DEV // PAGE
    pages = cache_rows.reshape(N_DP * N_MP, pages_dev, PAGE, 2 * KVH * HD)
    holders = page_table[:, 0].reshape(N_DP * N_MP, pages_dev)
    order = jnp.arange(pages_dev, dtype=jnp.int32)
    earlier = order[None, :] < order[:, None]
    rank = lax.optimization_barrier(jnp.sum(((holders[:, None, :] == holders[:, :, None]) & earlier[None]).astype(jnp.int32), axis=2)).astype(jnp.int32)
    device = jnp.arange(N_DP * N_MP, dtype=jnp.int32)
    source = jnp.broadcast_to((device // N_MP)[:, None], holders.shape)
    column = jnp.broadcast_to((device % N_MP)[:, None], holders.shape)
    page_cache = jnp.zeros((N_DP, N_MP, N_DP, PAGE_MOST, PAGE, 2 * KVH * HD), jnp.bfloat16)
    page_cache = page_cache.at[holders, column, source, rank].set(pages)
    return (layer_out, page_cache)
```

```python
import functools
import math

import jax
import jax.numpy as jnp
from jax import lax
from jax.experimental import pallas as pl
from jax.experimental.pallas import tpu as pltpu
from jax.sharding import PartitionSpec as P

MESH = pl.DeviceIdType.MESH
BF = jnp.bfloat16
F32 = jnp.float32
NDP = 8
NMP = 16
TD = 128
D = 2048
HB = 1024
NEG = -1e30
ANY = pl.BlockSpec(memory_space=pl.ANY)
VM = pl.BlockSpec(memory_space=pltpu.VMEM)
SM = pl.BlockSpec(memory_space=pltpu.SMEM)
VLIM = 62 * 1024 * 1024


def place():
    dp = lax.axis_index("dp")
    mp = lax.axis_index("mp")
    return dp, mp, lax.div(mp, 2), lax.rem(mp, 2)


def greet(peers):
    barrier = pltpu.get_barrier_semaphore()
    for peer in peers:
        pl.semaphore_signal(barrier, inc=1, device_id=peer, device_id_type=MESH)
    return barrier, len(peers)


def send(src, dst, ssem, rsem, dev):
    copy = pltpu.make_async_remote_copy(
        src_ref=src, dst_ref=dst, send_sem=ssem, recv_sem=rsem, device_id=dev, device_id_type=MESH
    )
    return copy


def landed(dst, ssem, rsem, dev):
    send(dst, dst, ssem, rsem, dev).wait_recv()


def norm_rows(x, gain):
    ms = jnp.mean(x * x, axis=-1, keepdims=True)
    return x * lax.rsqrt(ms + 1e-05) * gain


def front(
    tok, gain, wq, wkv, gate, up, down, valid,
    qkv_in, flag_in, wg, wu, wd, kvrows,
    wv, normed, cs, sbuf, fbuf, gs, us, dbf, kbuf, vbuf,
    wsem, qs, qr, fs, fr, gsend, grecv, usend, urecv, lsem,
):
    dp, mp, chip, core = place()
    others = [lax.rem(mp + s, NMP) for s in range(1, NMP)]
    barrier, count = greet([{"mp": j} for j in others])
    wcopies = []
    for n in range(6):
        src = wkv.at[:, pl.ds((n - 4) * 512, 512)] if n >= 4 else wq.at[:, pl.ds(n * 512, 512)]
        wcopies.append(pltpu.make_async_copy(src, wv.at[n], wsem.at[n]))
    order = (4, 5, 0, 1, 2, 3)
    for n in order:
        wcopies[n].start()
    for c in range(8):
        for i in range(8):
            cols = slice((i * 8 + c) * 128, (i * 8 + c + 1) * 128)
            gs[c, :, i * 128 : (i + 1) * 128] = gate[:, cols].astype(BF)
            us[c, :, i * 128 : (i + 1) * 128] = up[:, cols].astype(BF)
    dbf[...] = down[...].astype(BF)
    fbuf[...] = jnp.broadcast_to(valid[...].astype(F32), (16, TD)).astype(BF)
    local = [
        pltpu.make_async_copy(gs.at[chip], wg.at[dp, chip, core], lsem.at[0]),
        pltpu.make_async_copy(us.at[chip], wu.at[dp, chip, core], lsem.at[1]),
        pltpu.make_async_copy(dbf, wd.at[dp, core], lsem.at[2]),
        pltpu.make_async_copy(fbuf, flag_in.at[mp], lsem.at[3]),
    ]
    for copy in local:
        copy.start()
    pl.semaphore_wait(barrier, count)
    started = []
    for s in range(1, 8):
        c = lax.rem(chip + s, 8)
        dev = {"mp": c * 2 + core}
        for buf, out, ss, rs in ((gs, wg, gsend, grecv), (us, wu, usend, urecv)):
            copy = send(buf.at[c], out.at[dp, chip, core], ss.at[s], rs.at[s], dev)
            copy.start()
            started.append(copy)
    for s in range(1, NMP):
        copy = send(fbuf, flag_in.at[mp], fs.at[s], fr.at[s], {"mp": others[s - 1]})
        copy.start()
        started.append(copy)

    x = tok[...].astype(F32)
    normed[...] = norm_rows(x, gain[...]).astype(BF)
    lane = lax.broadcasted_iota(jnp.int32, (TD, 128), 1)
    row = lax.broadcasted_iota(jnp.int32, (TD, 128), 0) + mp * TD
    pos = row.astype(F32)
    freq = jnp.exp(lax.rem(lane, 32).astype(F32) * (-(2.0 / 64.0) * math.log(500000.0)))
    angle = pos * freq
    cs[0] = jnp.cos(angle)
    cs[1] = jnp.sin(angle)
    low = lane < 64
    first = lax.rem(lane, 64) < 32

    def turn(t):
        after = pltpu.roll(t, 96, 1)
        before = pltpu.roll(t, 32, 1)
        return t * cs[0] + jnp.where(first, -after, before) * cs[1]

    for n in order:
        wcopies[n].wait()
        acc = jnp.dot(normed[...], wv[n], preferred_element_type=F32)
        for l in range(4):
            t = acc[:, l * 128 : (l + 1) * 128]
            if n == 4:
                t = turn(t)
                kbuf[:, l * 128 : (l + 1) * 128] = t
                kvrows[:, l * 128 : (l + 1) * 128] = t.astype(BF)
            elif n == 5:
                vbuf[:, l * 128 : (l + 1) * 128] = t
                kvrows[:, 512 + l * 128 : 512 + (l + 1) * 128] = t.astype(BF)
            else:
                sbuf[n * 4 + l, 0] = (turn(t) * (0.125 * math.log2(math.e))).astype(BF)
        if n == 5:
            for l in range(4):
                kt = kbuf[:, l * 128 : (l + 1) * 128]
                vt = vbuf[:, l * 128 : (l + 1) * 128]
                even = jnp.where(low, kt, pltpu.roll(vt, 64, 1)).astype(BF)
                odd = jnp.where(low, pltpu.roll(kt, 64, 1), vt).astype(BF)
                sbuf[4 * l, 1] = even
                sbuf[4 * l + 1, 1] = even
                sbuf[4 * l + 2, 1] = odd
                sbuf[4 * l + 3, 1] = odd
    own = pltpu.make_async_copy(sbuf.at[mp], qkv_in.at[mp], lsem.at[4])
    own.start()
    for s in range(1, NMP):
        j = others[s - 1]
        copy = send(sbuf.at[j], qkv_in.at[mp], qs.at[s], qr.at[s], {"mp": j})
        copy.start()
        started.append(copy)
    own.wait()
    for copy in local:
        copy.wait()
    for copy in started:
        copy.wait_send()
    for s in range(1, 8):
        c = lax.rem(chip + 8 - s, 8)
        dev = {"mp": c * 2 + core}
        landed(wg.at[dp, c, core], gsend.at[s], grecv.at[s], dev)
        landed(wu.at[dp, c, core], usend.at[s], urecv.at[s], dev)
    for s in range(1, NMP):
        j = lax.rem(mp + NMP - s, NMP)
        landed(flag_in.at[j], fs.at[s], fr.at[s], {"mp": j})
        landed(qkv_in.at[j], qs.at[s], qr.at[s], {"mp": j})


def run_front(tok, gain, wq, wkv, gate, up, down, valid):
    sds = jax.ShapeDtypeStruct
    dma = pltpu.SemaphoreType.DMA
    return pl.pallas_call(
        front,
        out_shape=(
            sds((NMP, 2, TD, 128), BF),
            sds((NMP, 16, TD), BF),
            sds((8, 8, 2, 16, HB), BF),
            sds((8, 8, 2, 16, HB), BF),
            sds((8, 2, 64, D), BF),
            sds((TD, 1024), BF),
        ),
        in_specs=[VM, VM, ANY, ANY, VM, VM, VM, VM],
        out_specs=(ANY, ANY, ANY, ANY, ANY, VM),
        scratch_shapes=[
            pltpu.VMEM((6, D, 512), BF),
            pltpu.VMEM((TD, D), BF),
            pltpu.VMEM((2, TD, 128), F32),
            pltpu.VMEM((NMP, 2, TD, 128), BF),
            pltpu.VMEM((16, TD), BF),
            pltpu.VMEM((8, 16, HB), BF),
            pltpu.VMEM((8, 16, HB), BF),
            pltpu.VMEM((64, D), BF),
            pltpu.VMEM((TD, 512), F32),
            pltpu.VMEM((TD, 512), F32),
            dma((6,)), dma((NMP,)), dma((NMP,)), dma((NMP,)), dma((NMP,)),
            dma((8,)), dma((8,)), dma((8,)), dma((8,)), dma((5,)),
        ],
        compiler_params=pltpu.CompilerParams(
            collective_id=1, has_side_effects=True, vmem_limit_bytes=VLIM
        ),
        name="front",
    )(tok, gain, wq, wkv, gate, up, down, valid)


class Relay:
    def __init__(self, wg, wu, wd, ssem, rsem):
        self.wg, self.wu, self.wd, self.ssem, self.rsem = wg, wu, wd, ssem, rsem
        dp, mp, chip, core = place()
        z, xh = lax.div(dp, 2), lax.rem(dp, 2)
        self.core, self.xh = core, xh
        self.zm, self.zp, self.z2, self.z = lax.rem(z + 3, 4), lax.rem(z + 1, 4), lax.rem(z + 2, 4), z
        self.xo = 1 - xh
        self.partner = {"mp": chip * 2 + 1 - core}
        self.up = {"dp": self.zp * 2 + xh}
        self.down = {"dp": self.zm * 2 + xh}
        self.across = {"dp": z * 2 + self.xo}
        self.count = 0
        self.started = []

    def part(self, block, core, p):
        if p == 0:
            return self.wg.at[block, :, core]
        if p == 1:
            return self.wu.at[block, :, core]
        if p == 2:
            return self.wd.at[block, core, pl.ds(0, 32)]
        return self.wd.at[block, core, pl.ds(32, 32)]

    def put(self, block, parts, event, dev):
        for p in parts:
            ref = self.part(block, self.core, p)
            copy = send(ref, ref, self.ssem.at[self.count], self.rsem.at[event, p], dev)
            copy.start()
            self.started.append(copy)
            self.count += 1

    def got(self, block, parts, event, core=None):
        for p in parts:
            ref = self.part(block, self.core if core is None else core, p)
            landed(ref, self.ssem.at[0], self.rsem.at[event, p], self.partner)

    def finish(self):
        for copy in self.started:
            copy.wait_send()

    def stage0(self):
        b = self.z * 2 + self.xh
        self.put(b, (0, 1, 2, 3), 0, self.across)
        self.put(b, (0, 1, 2, 3), 1, self.up)
        self.put(b, (0, 1, 2, 3), 2, self.down)
        self.put(b, (0, 1, 2, 3), 8, self.partner)

    def stage1(self):
        b = self.z * 2 + self.xo
        self.got(b, (0, 1, 2, 3), 0)
        self.put(b, (0, 1, 2, 3), 3, self.up)
        self.put(b, (0, 1, 2, 3), 4, self.down)
        self.put(b, (0, 1, 2, 3), 9, self.partner)

    def stage2(self):
        b = self.zm * 2 + self.xh
        self.got(b, (0, 1, 2, 3), 1)
        self.put(b, (0, 2), 5, self.up)
        self.put(b, (0, 1, 2, 3), 10, self.partner)
        b = self.zp * 2 + self.xh
        self.got(b, (0, 1, 2, 3), 2)
        self.put(b, (1, 3), 5, self.down)
        self.put(b, (0, 1, 2, 3), 11, self.partner)

    def stage3(self):
        b = self.zm * 2 + self.xo
        self.got(b, (0, 1, 2, 3), 3)
        self.put(b, (0, 2), 6, self.up)
        self.put(b, (0, 1, 2, 3), 12, self.partner)
        b = self.zp * 2 + self.xo
        self.got(b, (0, 1, 2, 3), 4)
        self.put(b, (1, 3), 6, self.down)
        self.put(b, (0, 1, 2, 3), 13, self.partner)

    def stage4(self):
        b = self.z2 * 2 + self.xh
        self.got(b, (0, 1, 2, 3), 5)
        self.put(b, (0, 1, 2, 3), 14, self.partner)
        b = self.z2 * 2 + self.xo
        self.got(b, (0, 1, 2, 3), 6)
        self.put(b, (0, 1, 2, 3), 15, self.partner)

    def stage5(self):
        blocks = (
            self.z * 2 + self.xh, self.z * 2 + self.xo, self.zm * 2 + self.xh, self.zp * 2 + self.xh,
            self.zm * 2 + self.xo, self.zp * 2 + self.xo, self.z2 * 2 + self.xh, self.z2 * 2 + self.xo,
        )
        for e, b in enumerate(blocks):
            self.got(b, (0, 1, 2, 3), 8 + e, 1 - self.core)


def attend(
    qkv, flags, kvrows, lens, table, wg_i, wu_i, wd_i,
    att_in, cache, wg, wu, wd,
    qa, ka, va, fb, tile, pbuf, m_s, acc_s,
    ssem, rsem, asend, arecv, psend, precv, lsem,
):
    dp, mp, chip, core = place()
    others = [lax.rem(mp + s, NMP) for s in range(1, NMP)]
    dothers = [lax.rem(dp + s, NDP) for s in range(1, NDP)]
    barrier, count = greet([{"mp": j} for j in others] + [{"dp": i} for i in dothers])
    relay = Relay(wg, wu, wd, ssem, rsem)
    length = lens[0, 0]

    holder = [table[p, 0] for p in range(8)]
    target = []
    for p in range(8):
        rank = jnp.int32(0)
        for q in range(p):
            rank = rank + jnp.where(holder[q] == holder[p], 1, 0)
        target.append(holder[p] * 2 + rank)
    col = lax.broadcasted_iota(jnp.int32, (256, 128), 1)
    row = lax.broadcasted_iota(jnp.int32, (256, 128), 0)
    want = jnp.zeros((256, 128), jnp.int32)
    for p in range(8):
        want = jnp.where(lax.div(col, 16) == p, target[p], want)
    pick = (lax.div(row, 16) == want) & (lax.rem(row, 16) == lax.rem(col, 16))
    pick = jnp.where(pick, 1.0, 0.0).astype(BF)
    pages = jnp.dot(pick, kvrows[...], preferred_element_type=F32).astype(BF)
    for i in range(8):
        for r in range(2):
            pbuf[i, r] = pages[(i * 2 + r) * 16 : (i * 2 + r + 1) * 16]

    pl.semaphore_wait(barrier, count)
    relay.stage0()
    started = []
    own_pages = pltpu.make_async_copy(pbuf.at[dp], cache.at[dp], lsem.at[0])
    own_pages.start()
    for s in range(1, NDP):
        i = dothers[s - 1]
        copy = send(pbuf.at[i], cache.at[dp], psend.at[s], precv.at[s], {"dp": i})
        copy.start()
        started.append(copy)

    lane = lax.broadcasted_iota(jnp.int32, (TD, 128), 1)
    sub = lax.broadcasted_iota(jnp.int32, (TD, 128), 0)
    low = lane < 64

    def prepare(b, carry):
        q = qkv[b, 0].astype(F32)
        kv = qkv[b, 1].astype(F32)
        frow = flags[b].astype(F32)[0:1, :]
        token = sub + b * TD
        late = jnp.where(token >= length, 1.0, 0.0)
        extra = jnp.where(lane == 64, 1.0, jnp.where(lane == 65, late, 0.0))
        qi, half = lax.div(b, 2), lax.rem(b, 2)
        qa[qi, pl.ds(half * TD, TD), :] = jnp.where(low, q, extra).astype(BF)
        qa[qi, pl.ds(256 + half * TD, TD), :] = jnp.where(low, pltpu.roll(q, 64, 1), extra).astype(BF)
        fcol = jnp.sum(jnp.where(lane == sub, frow, 0.0), axis=1, keepdims=True)
        closed = jnp.where(fcol > 0.5, 0.0, NEG)
        early = jnp.where(token >= length, 0.0, NEG)
        bias = jnp.where(lane == 64, closed, jnp.where(lane == 65, early, 0.0))
        ka[qi, pl.ds(half * TD, TD), :] = jnp.where(low, kv, bias).astype(BF)
        one = jnp.where(lane == 64, 1.0, 0.0)
        va[qi, pl.ds(half * TD, TD), :] = jnp.where(low, pltpu.roll(kv, 64, 1), one).astype(BF)
        fb[b] = jnp.broadcast_to(frow, (8, TD))
        return carry

    lax.fori_loop(0, NMP, prepare, 0)

    trow = lax.broadcasted_iota(jnp.int32, (512, 256), 0)
    trow = lax.rem(trow, 256)
    tcol = lax.broadcasted_iota(jnp.int32, (512, 256), 1)
    nt = (((1,), (1,)), ((), ()))
    qlane = lax.broadcasted_iota(jnp.int32, (512, 128), 1)
    hlane = lax.broadcasted_iota(jnp.int32, (256, 128), 1)

    def block(qi, carry):
        q = qa[qi]
        bare = jnp.where(qlane < 64, q.astype(F32), 0.0).astype(BF)
        s = lax.dot_general(bare, ka[qi], nt, preferred_element_type=F32)
        open_row = jnp.concatenate([fb[2 * qi][0:1], fb[2 * qi + 1][0:1]], axis=1) > 0.5
        base = qi * 256
        split = (trow + base >= length) & (tcol + base < length)
        ok = ((tcol < trow) & open_row & jnp.logical_not(split)) | (tcol == trow)
        s = jnp.where(ok, s, NEG)
        m = jnp.max(s, axis=1, keepdims=True)
        p = jnp.exp2(s - m)
        acc = jnp.dot(p.astype(BF), va[qi], preferred_element_type=F32)
        m_s[...] = m
        acc_s[...] = acc

        def step(ki, c2):
            s = lax.dot_general(qa[qi], ka[ki], nt, preferred_element_type=F32)
            m = m_s[...]
            m_new = jnp.maximum(m, jnp.max(s, axis=1, keepdims=True))
            p = jnp.exp2(s - m_new)
            acc_s[...] = acc_s[...] * jnp.exp2(m - m_new) + jnp.dot(
                p.astype(BF), va[ki], preferred_element_type=F32
            )
            m_s[...] = m_new
            return c2

        lax.fori_loop(0, qi, step, 0)
        acc = acc_s[...]
        out = acc / acc[:, 64:65]
        both = jnp.where(hlane < 64, out[:256], pltpu.roll(out[256:], 64, 1)).astype(BF)
        for half in range(2):
            j = 2 * qi + half
            tile[j] = both[half * TD : (half + 1) * TD]

            @pl.when(j != mp)
            def _():
                send(tile.at[j], att_in.at[mp], asend.at[j], arecv.at[mp], {"mp": j}).start()

            @pl.when(j == mp)
            def _():
                pltpu.make_async_copy(tile.at[j], att_in.at[j], lsem.at[1]).start()

        return carry

    lax.fori_loop(0, 4, block, 0)
    relay.stage1()
    lax.fori_loop(4, 8, block, 0)
    relay.stage2()
    relay.stage3()
    relay.stage4()
    relay.stage5()
    pltpu.make_async_copy(tile.at[mp], att_in.at[mp], lsem.at[1]).wait()
    for s in range(1, NMP):
        j = others[s - 1]
        copy = send(tile.at[j], att_in.at[j], asend.at[j], arecv.at[j], {"mp": j})
        copy.wait_send()
        copy.wait_recv()
    own_pages.wait()
    for s in range(1, NDP):
        started[s - 1].wait_send()
        i = lax.rem(dp + NDP - s, NDP)
        landed(cache.at[i], psend.at[s], precv.at[s], {"dp": i})
    relay.finish()


def run_attend(qkv, flags, kvrows, lens, table, wg, wu, wd):
    sds = jax.ShapeDtypeStruct
    dma = pltpu.SemaphoreType.DMA
    return pl.pallas_call(
        attend,
        out_shape=(
            sds((NMP, TD, 128), BF),
            sds((NDP, 2, 16, 1024), BF),
            sds(wg.shape, BF),
            sds(wu.shape, BF),
            sds(wd.shape, BF),
        ),
        in_specs=[VM, VM, VM, SM, SM, ANY, ANY, ANY],
        out_specs=(ANY, ANY, ANY, ANY, ANY),
        input_output_aliases={5: 2, 6: 3, 7: 4},
        scratch_shapes=[
            pltpu.VMEM((8, 512, 128), BF),
            pltpu.VMEM((8, 256, 128), BF),
            pltpu.VMEM((8, 256, 128), BF),
            pltpu.VMEM((NMP, 8, TD), F32),
            pltpu.VMEM((NMP, TD, 128), BF),
            pltpu.VMEM((NDP, 2, 16, 1024), BF),
            pltpu.VMEM((512, 1), F32),
            pltpu.VMEM((512, 128), F32),
            dma((72,)), dma((16, 4)), dma((NMP,)), dma((NMP,)), dma((NDP,)), dma((NDP,)), dma((2,)),
        ],
        compiler_params=pltpu.CompilerParams(
            collective_id=2, has_side_effects=True, vmem_limit_bytes=VLIM
        ),
        name="attend",
    )(qkv, flags, kvrows, lens, table, wg, wu, wd)


def mlp(
    att, tok, gain, wo, wg, wu, wd,
    out,
    att_v, wo_v, wg_v, wu_v, wd_v, hid, act, hbuf, part, rs,
    wsem, gs, gr, ss, sr,
):
    dp, mp, chip, core = place()
    y, x = lax.div(chip, 2), lax.rem(chip, 2)
    yp, ym, y2, xo = lax.rem(y + 1, 4), lax.rem(y + 3, 4), lax.rem(y + 2, 4), 1 - x

    def dev(yy, xx):
        return {"mp": (yy * 2 + xx) * 2 + core}

    peers = [(y, xo), (yp, x), (ym, x), (yp, xo), (ym, xo), (y2, x), (y2, xo)]
    barrier, count = greet([dev(*p) for p in peers])
    loads = [
        pltpu.make_async_copy(wo, wo_v, wsem.at[0]),
        pltpu.make_async_copy(wg, wg_v, wsem.at[1]),
        pltpu.make_async_copy(wu, wu_v, wsem.at[2]),
        pltpu.make_async_copy(wd, wd_v, wsem.at[3]),
    ]
    for copy in loads:
        copy.start()
    for j in range(NMP):
        att_v[:, j * 128 : (j + 1) * 128] = att[j]
    loads[0].wait()

    def project(n, carry):
        cols = pl.ds(pl.multiple_of(n * 512, 512), 512)
        got = jnp.dot(att_v[...], wo_v[:, cols], preferred_element_type=F32)
        hid[:, cols] = (tok[:, cols].astype(F32) + got).astype(BF).astype(F32)
        return carry

    lax.fori_loop(0, 4, project, 0)
    act[chip] = norm_rows(hid[...], gain[...]).astype(BF)
    pl.semaphore_wait(barrier, count)

    started = []
    half = (pl.ds(0, 64), pl.ds(64, 64))

    def forward(block, rows, event, to):
        ref = act.at[block] if rows is None else act.at[block, rows]
        copy = send(ref, ref, gs.at[len(started)], gr.at[event], dev(*to))
        copy.start()
        started.append(copy)

    def arrive(block, rows, event):
        ref = act.at[block] if rows is None else act.at[block, rows]
        landed(ref, gs.at[0], gr.at[event], dev(y, xo))

    def slot(yy, xx):
        return yy * 2 + xx

    mine = slot(y, x)
    forward(mine, None, 0, (y, xo))
    forward(mine, None, 1, (yp, x))
    forward(mine, None, 2, (ym, x))
    arrive(slot(y, xo), None, 0)
    forward(slot(y, xo), None, 3, (yp, x))
    forward(slot(y, xo), None, 4, (ym, x))
    arrive(slot(ym, x), None, 1)
    forward(slot(ym, x), half[0], 5, (yp, x))
    arrive(slot(yp, x), None, 2)
    forward(slot(yp, x), half[1], 6, (ym, x))
    for copy in loads[1:]:
        copy.wait()

    sends = []

    def pair(yy):
        rows = act.at[pl.ds(yy * 2, 2)]
        w_g = wg_v
        w_u = wu_v

        def hidden(n, carry):
            cols = pl.ds(pl.multiple_of(n * 256, 256), 256)
            xin = rows[...].reshape(256, D)
            g = jnp.dot(xin, w_g[:, cols], preferred_element_type=F32)
            u = jnp.dot(xin, w_u[:, cols], preferred_element_type=F32)
            hbuf[:, cols] = (g / (1.0 + jnp.exp(-g)) * u).astype(BF)
            return carry

        lax.fori_loop(0, 4, hidden, 0)

        def final(n, carry):
            cols = pl.ds(pl.multiple_of(n * 512, 512), 512)
            r = jnp.dot(hbuf[...], wd_v[:, cols], preferred_element_type=F32).astype(BF)
            part[yy * 2, :, cols] = r[:TD]
            part[yy * 2 + 1, :, cols] = r[TD:]
            return carry

        lax.fori_loop(0, 4, final, 0)

    def give(yy, xx, event):
        copy = send(part.at[slot(yy, xx)], rs.at[mine], ss.at[event], sr.at[event], dev(yy, xx))
        copy.start()
        sends.append(copy)

    pair(y)
    give(y, xo, 0)
    arrive(slot(ym, xo), None, 3)
    forward(slot(ym, xo), half[0], 7, (yp, x))
    arrive(slot(yp, xo), None, 4)
    forward(slot(yp, xo), half[1], 8, (ym, x))
    pair(ym)
    give(ym, x, 1)
    give(ym, xo, 2)
    pair(yp)
    give(yp, x, 3)
    give(yp, xo, 4)
    arrive(slot(y2, x), half[0], 5)
    arrive(slot(y2, x), half[1], 6)
    arrive(slot(y2, xo), half[0], 7)
    arrive(slot(y2, xo), half[1], 8)
    pair(y2)
    give(y2, x, 5)
    give(y2, xo, 6)
    for event, src in enumerate([(y, xo), (yp, x), (yp, xo), (ym, x), (ym, xo), (y2, x), (y2, xo)]):
        landed(rs.at[slot(*src)], ss.at[event], sr.at[event], dev(*src))
    rs[mine] = part[mine]

    def close(n, carry):
        cols = pl.ds(pl.multiple_of(n * 256, 256), 256)
        total = rs[0, :, cols].astype(F32)
        for c in range(1, 8):
            total = total + rs[c, :, cols].astype(F32)
        out[:, cols] = (hid[:, cols] + total).astype(BF)
        return carry

    lax.fori_loop(0, 8, close, 0)
    for copy in started + sends:
        copy.wait_send()


def run_mlp(att, tok, gain, wo, wg, wu, wd):
    dma = pltpu.SemaphoreType.DMA
    return pl.pallas_call(
        mlp,
        out_shape=jax.ShapeDtypeStruct((TD, D), BF),
        in_specs=[VM, VM, VM, ANY, ANY, ANY, ANY],
        out_specs=VM,
        scratch_shapes=[
            pltpu.VMEM((TD, D), BF),
            pltpu.VMEM((D, D), BF),
            pltpu.VMEM((D, HB), BF),
            pltpu.VMEM((D, HB), BF),
            pltpu.VMEM((HB, D), BF),
            pltpu.VMEM((TD, D), F32),
            pltpu.VMEM((8, TD, D), BF),
            pltpu.VMEM((256, HB), BF),
            pltpu.VMEM((8, TD, D), BF),
            pltpu.VMEM((8, TD, D), BF),
            dma((4,)), dma((9,)), dma((9,)), dma((7,)), dma((7,)),
        ],
        compiler_params=pltpu.CompilerParams(
            collective_id=3, has_side_effects=True, vmem_limit_bytes=VLIM
        ),
        name="mlp",
    )(att, tok, gain, wo, wg, wu, wd)


def on_device(
    tokens, attn_gain, mlp_gain, query_weight, keyval_weight, output_weight,
    gate_rows, up_rows, down_rows, lengths, valid, page_table,
):
    qkv, flags, wg, wu, wd, kvrows = run_front(
        tokens, attn_gain.reshape(1, D), query_weight, keyval_weight,
        gate_rows, up_rows, down_rows, valid.reshape(1, TD),
    )
    att, cache, wg, wu, wd = run_attend(qkv, flags, kvrows, lengths, page_table, wg, wu, wd)
    layer_out = run_mlp(
        att, tokens, mlp_gain.reshape(1, D), output_weight,
        wg.reshape(D, HB), wu.reshape(D, HB), wd.reshape(HB, D),
    )
    return (layer_out, cache[None, None])


def solution(mesh):
    return jax.shard_map(
        on_device,
        mesh=mesh,
        in_specs=(
            P(("dp", "mp"), None), P(), P(), P(), P(), P(),
            P(("dp", "mp"), None), P(("dp", "mp"), None), P(("dp", "mp"), None),
            P("dp", None), P(("dp", "mp")), P(("dp", "mp"), None),
        ),
        out_specs=(P(("dp", "mp"), None), P("dp", "mp", None, None, None, None)),
        check_vma=False,
    )
```

```python
import functools
import math

import jax
import jax.numpy as jnp
from jax import lax
from jax.experimental import pallas as pl
from jax.experimental.pallas import tpu as pltpu
from jax.sharding import PartitionSpec as P

MESH = pl.DeviceIdType.MESH
BF = jnp.bfloat16
F32 = jnp.float32
NDP = 8
NMP = 16
TD = 128
D = 2048
HB = 1024
NEG = -1e30
ANY = pl.BlockSpec(memory_space=pl.ANY)
VM = pl.BlockSpec(memory_space=pltpu.VMEM)
SM = pl.BlockSpec(memory_space=pltpu.SMEM)
VLIM = 62 * 1024 * 1024


def place():
    dp = lax.axis_index("dp")
    mp = lax.axis_index("mp")
    return dp, mp, lax.div(mp, 2), lax.rem(mp, 2)


def greet(peers):
    barrier = pltpu.get_barrier_semaphore()
    for peer in peers:
        pl.semaphore_signal(barrier, inc=1, device_id=peer, device_id_type=MESH)
    return barrier, len(peers)


def send(src, dst, ssem, rsem, dev):
    copy = pltpu.make_async_remote_copy(
        src_ref=src, dst_ref=dst, send_sem=ssem, recv_sem=rsem, device_id=dev, device_id_type=MESH
    )
    return copy


def landed(dst, ssem, rsem, dev):
    send(dst, dst, ssem, rsem, dev).wait_recv()


def norm_rows(x, gain):
    ms = jnp.mean(x * x, axis=-1, keepdims=True)
    return x * lax.rsqrt(ms + 1e-05) * gain


def front(
    tok, gain, wq, wkv, gate, up, down, valid,
    qkv_in, flag_in, wg, wu, wd, kvrows,
    wv, normed, cs, sbuf, fbuf, gs, us, kbuf, vbuf,
    wsem, qs, qr, fs, fr, gsend, grecv, usend, urecv, lsem,
):
    dp, mp, chip, core = place()
    others = [lax.rem(mp + s, NMP) for s in range(1, NMP)]
    barrier, count = greet([{"mp": j} for j in others])
    wcopies = []
    for n in range(6):
        src = wkv.at[:, pl.ds((n - 4) * 512, 512)] if n >= 4 else wq.at[:, pl.ds(n * 512, 512)]
        wcopies.append(pltpu.make_async_copy(src, wv.at[n], wsem.at[n]))
    order = (4, 5, 0, 1, 2, 3)
    for n in order:
        wcopies[n].start()
    for c in range(8):
        for i in range(8):
            cols = slice((i * 8 + c) * 128, (i * 8 + c + 1) * 128)
            gs[c, :, i * 128 : (i + 1) * 128] = gate[:, cols].astype(BF)
            us[c, :, i * 128 : (i + 1) * 128] = up[:, cols].astype(BF)
    wd[...] = down[...].astype(BF)
    fbuf[...] = jnp.broadcast_to(valid[...].astype(F32), (16, TD)).astype(BF)
    local = [
        pltpu.make_async_copy(gs.at[chip], wg.at[dp, chip, core], lsem.at[0]),
        pltpu.make_async_copy(us.at[chip], wu.at[dp, chip, core], lsem.at[1]),
        pltpu.make_async_copy(fbuf, flag_in.at[mp], lsem.at[2]),
    ]
    for copy in local:
        copy.start()
    pl.semaphore_wait(barrier, count)
    started = []
    for s in range(1, 8):
        c = lax.rem(chip + s, 8)
        dev = {"mp": c * 2 + core}
        for buf, out, ss, rs in ((gs, wg, gsend, grecv), (us, wu, usend, urecv)):
            copy = send(buf.at[c], out.at[dp, chip, core], ss.at[s], rs.at[s], dev)
            copy.start()
            started.append(copy)
    for s in range(1, NMP):
        copy = send(fbuf, flag_in.at[mp], fs.at[s], fr.at[s], {"mp": others[s - 1]})
        copy.start()
        started.append(copy)

    x = tok[...].astype(F32)
    normed[...] = norm_rows(x, gain[...]).astype(BF)
    lane = lax.broadcasted_iota(jnp.int32, (TD, 128), 1)
    row = lax.broadcasted_iota(jnp.int32, (TD, 128), 0) + mp * TD
    pos = row.astype(F32)
    freq = jnp.exp(lax.rem(lane, 32).astype(F32) * (-(2.0 / 64.0) * math.log(500000.0)))
    angle = pos * freq
    cs[0] = jnp.cos(angle)
    cs[1] = jnp.sin(angle)
    low = lane < 64
    first = lax.rem(lane, 64) < 32

    def turn(t):
        after = pltpu.roll(t, 96, 1)
        before = pltpu.roll(t, 32, 1)
        return t * cs[0] + jnp.where(first, -after, before) * cs[1]

    for n in order:
        wcopies[n].wait()
        acc = jnp.dot(normed[...], wv[n], preferred_element_type=F32)
        for l in range(4):
            t = acc[:, l * 128 : (l + 1) * 128]
            if n == 4:
                t = turn(t)
                kbuf[:, l * 128 : (l + 1) * 128] = t
                kvrows[:, l * 128 : (l + 1) * 128] = t.astype(BF)
            elif n == 5:
                vbuf[:, l * 128 : (l + 1) * 128] = t
                kvrows[:, 512 + l * 128 : 512 + (l + 1) * 128] = t.astype(BF)
            else:
                sbuf[n * 4 + l, 0] = (turn(t) * (0.125 * math.log2(math.e))).astype(BF)
        if n == 5:
            for l in range(4):
                kt = kbuf[:, l * 128 : (l + 1) * 128]
                vt = vbuf[:, l * 128 : (l + 1) * 128]
                even = jnp.where(low, kt, pltpu.roll(vt, 64, 1)).astype(BF)
                odd = jnp.where(low, pltpu.roll(kt, 64, 1), vt).astype(BF)
                sbuf[4 * l, 1] = even
                sbuf[4 * l + 1, 1] = even
                sbuf[4 * l + 2, 1] = odd
                sbuf[4 * l + 3, 1] = odd
    own = pltpu.make_async_copy(sbuf.at[mp], qkv_in.at[mp], lsem.at[3])
    own.start()
    for s in range(1, NMP):
        j = others[s - 1]
        copy = send(sbuf.at[j], qkv_in.at[mp], qs.at[s], qr.at[s], {"mp": j})
        copy.start()
        started.append(copy)
    own.wait()
    for copy in local:
        copy.wait()
    for copy in started:
        copy.wait_send()
    for s in range(1, 8):
        c = lax.rem(chip + 8 - s, 8)
        dev = {"mp": c * 2 + core}
        landed(wg.at[dp, c, core], gsend.at[s], grecv.at[s], dev)
        landed(wu.at[dp, c, core], usend.at[s], urecv.at[s], dev)
    for s in range(1, NMP):
        j = lax.rem(mp + NMP - s, NMP)
        landed(flag_in.at[j], fs.at[s], fr.at[s], {"mp": j})
        landed(qkv_in.at[j], qs.at[s], qr.at[s], {"mp": j})


def run_front(tok, gain, wq, wkv, gate, up, down, valid):
    sds = jax.ShapeDtypeStruct
    dma = pltpu.SemaphoreType.DMA
    return pl.pallas_call(
        front,
        out_shape=(
            sds((NMP, 2, TD, 128), BF),
            sds((NMP, 16, TD), BF),
            sds((8, 8, 2, 16, HB), BF),
            sds((8, 8, 2, 16, HB), BF),
            sds((64, D), BF),
            sds((TD, 1024), BF),
        ),
        in_specs=[VM, VM, ANY, ANY, VM, VM, VM, VM],
        out_specs=(ANY, ANY, ANY, ANY, VM, VM),
        scratch_shapes=[
            pltpu.VMEM((6, D, 512), BF),
            pltpu.VMEM((TD, D), BF),
            pltpu.VMEM((2, TD, 128), F32),
            pltpu.VMEM((NMP, 2, TD, 128), BF),
            pltpu.VMEM((16, TD), BF),
            pltpu.VMEM((8, 16, HB), BF),
            pltpu.VMEM((8, 16, HB), BF),
            pltpu.VMEM((TD, 512), F32),
            pltpu.VMEM((TD, 512), F32),
            dma((6,)), dma((NMP,)), dma((NMP,)), dma((NMP,)), dma((NMP,)),
            dma((8,)), dma((8,)), dma((8,)), dma((8,)), dma((4,)),
        ],
        compiler_params=pltpu.CompilerParams(
            collective_id=1, has_side_effects=True, vmem_limit_bytes=VLIM
        ),
        name="front",
    )(tok, gain, wq, wkv, gate, up, down, valid)


class Relay:
    def __init__(self, part, ssem, rsem):
        self.part, self.ssem, self.rsem = part, ssem, rsem
        dp, mp, chip, core = place()
        z, xh = lax.div(dp, 2), lax.rem(dp, 2)
        self.core, self.xh = core, xh
        self.zm, self.zp, self.z2, self.z = lax.rem(z + 3, 4), lax.rem(z + 1, 4), lax.rem(z + 2, 4), z
        self.xo = 1 - xh
        self.partner = {"mp": chip * 2 + 1 - core}
        self.up = {"dp": self.zp * 2 + xh}
        self.down = {"dp": self.zm * 2 + xh}
        self.across = {"dp": z * 2 + self.xo}
        self.count = 0
        self.started = []

    def put(self, block, parts, event, dev):
        for p in parts:
            ref = self.part(block, self.core, p)
            copy = send(ref, ref, self.ssem.at[self.count], self.rsem.at[event, p], dev)
            copy.start()
            self.started.append(copy)
            self.count += 1

    def got(self, block, parts, event, core=None):
        for p in parts:
            ref = self.part(block, self.core if core is None else core, p)
            landed(ref, self.ssem.at[0], self.rsem.at[event, p], self.partner)

    def finish(self):
        for copy in self.started:
            copy.wait_send()

    def stage0(self):
        b = self.z * 2 + self.xh
        self.put(b, (0, 1), 0, self.across)
        self.put(b, (0, 1), 1, self.up)
        self.put(b, (0, 1), 2, self.down)
        self.put(b, (0, 1), 8, self.partner)

    def stage1(self):
        b = self.z * 2 + self.xo
        self.got(b, (0, 1), 0)
        self.put(b, (0, 1), 3, self.up)
        self.put(b, (0, 1), 4, self.down)
        self.put(b, (0, 1), 9, self.partner)

    def stage2(self):
        b = self.zm * 2 + self.xh
        self.got(b, (0, 1), 1)
        self.put(b, (0,), 5, self.up)
        self.put(b, (0, 1), 10, self.partner)
        b = self.zp * 2 + self.xh
        self.got(b, (0, 1), 2)
        self.put(b, (1,), 5, self.down)
        self.put(b, (0, 1), 11, self.partner)

    def stage3(self):
        b = self.zm * 2 + self.xo
        self.got(b, (0, 1), 3)
        self.put(b, (0,), 6, self.up)
        self.put(b, (0, 1), 12, self.partner)
        b = self.zp * 2 + self.xo
        self.got(b, (0, 1), 4)
        self.put(b, (1,), 6, self.down)
        self.put(b, (0, 1), 13, self.partner)

    def stage4(self):
        b = self.z2 * 2 + self.xh
        self.got(b, (0, 1), 5)
        self.put(b, (0, 1), 14, self.partner)
        b = self.z2 * 2 + self.xo
        self.got(b, (0, 1), 6)
        self.put(b, (0, 1), 15, self.partner)

    def stage5(self):
        blocks = (
            self.z * 2 + self.xh, self.z * 2 + self.xo, self.zm * 2 + self.xh, self.zp * 2 + self.xh,
            self.zm * 2 + self.xo, self.zp * 2 + self.xo, self.z2 * 2 + self.xh, self.z2 * 2 + self.xo,
        )
        for e, b in enumerate(blocks):
            self.got(b, (0, 1), 8 + e, 1 - self.core)


def attend(
    qkv, flags, kvrows, lens, table, wg_i, wu_i,
    att_in, cache, wg, wu,
    qa, ka, va, fb, tile, pbuf, m_s, acc_s,
    ssem, rsem, asend, arecv, psend, precv, lsem,
):
    dp, mp, chip, core = place()
    others = [lax.rem(mp + s, NMP) for s in range(1, NMP)]
    dothers = [lax.rem(dp + s, NDP) for s in range(1, NDP)]
    barrier, count = greet([{"mp": j} for j in others] + [{"dp": i} for i in dothers])
    relay = Relay(lambda b, c, p: (wg, wu)[p].at[b, :, c], ssem, rsem)
    length = lens[0, 0]

    holder = [table[p, 0] for p in range(8)]
    target = []
    for p in range(8):
        rank = jnp.int32(0)
        for q in range(p):
            rank = rank + jnp.where(holder[q] == holder[p], 1, 0)
        target.append(holder[p] * 2 + rank)
    col = lax.broadcasted_iota(jnp.int32, (256, 128), 1)
    row = lax.broadcasted_iota(jnp.int32, (256, 128), 0)
    want = jnp.zeros((256, 128), jnp.int32)
    for p in range(8):
        want = jnp.where(lax.div(col, 16) == p, target[p], want)
    pick = (lax.div(row, 16) == want) & (lax.rem(row, 16) == lax.rem(col, 16))
    pick = jnp.where(pick, 1.0, 0.0).astype(BF)
    pages = jnp.dot(pick, kvrows[...], preferred_element_type=F32).astype(BF)
    for i in range(8):
        for r in range(2):
            pbuf[i, r] = pages[(i * 2 + r) * 16 : (i * 2 + r + 1) * 16]

    pl.semaphore_wait(barrier, count)
    relay.stage0()
    started = []
    own_pages = pltpu.make_async_copy(pbuf.at[dp], cache.at[dp], lsem.at[0])
    own_pages.start()
    for s in range(1, NDP):
        i = dothers[s - 1]
        copy = send(pbuf.at[i], cache.at[dp], psend.at[s], precv.at[s], {"dp": i})
        copy.start()
        started.append(copy)

    lane = lax.broadcasted_iota(jnp.int32, (TD, 128), 1)
    sub = lax.broadcasted_iota(jnp.int32, (TD, 128), 0)
    low = lane < 64

    def prepare(b, carry):
        q = qkv[b, 0].astype(F32)
        kv = qkv[b, 1].astype(F32)
        frow = flags[b].astype(F32)[0:1, :]
        token = sub + b * TD
        late = jnp.where(token >= length, 1.0, 0.0)
        extra = jnp.where(lane == 64, 1.0, jnp.where(lane == 65, late, 0.0))
        qi, half = lax.div(b, 2), lax.rem(b, 2)
        qa[qi, pl.ds(half * TD, TD), :] = jnp.where(low, q, extra).astype(BF)
        qa[qi, pl.ds(256 + half * TD, TD), :] = jnp.where(low, pltpu.roll(q, 64, 1), extra).astype(BF)
        fcol = jnp.sum(jnp.where(lane == sub, frow, 0.0), axis=1, keepdims=True)
        closed = jnp.where(fcol > 0.5, 0.0, NEG)
        early = jnp.where(token >= length, 0.0, NEG)
        bias = jnp.where(lane == 64, closed, jnp.where(lane == 65, early, 0.0))
        ka[qi, pl.ds(half * TD, TD), :] = jnp.where(low, kv, bias).astype(BF)
        one = jnp.where(lane == 64, 1.0, 0.0)
        va[qi, pl.ds(half * TD, TD), :] = jnp.where(low, pltpu.roll(kv, 64, 1), one).astype(BF)
        fb[b] = jnp.broadcast_to(frow, (8, TD))
        return carry

    lax.fori_loop(0, NMP, prepare, 0)

    trow = lax.broadcasted_iota(jnp.int32, (512, 256), 0)
    trow = lax.rem(trow, 256)
    tcol = lax.broadcasted_iota(jnp.int32, (512, 256), 1)
    nt = (((1,), (1,)), ((), ()))
    qlane = lax.broadcasted_iota(jnp.int32, (512, 128), 1)
    hlane = lax.broadcasted_iota(jnp.int32, (256, 128), 1)

    def block(qi, carry):
        q = qa[qi]
        bare = jnp.where(qlane < 64, q.astype(F32), 0.0).astype(BF)
        s = lax.dot_general(bare, ka[qi], nt, preferred_element_type=F32)
        open_row = jnp.concatenate([fb[2 * qi][0:1], fb[2 * qi + 1][0:1]], axis=1) > 0.5
        base = qi * 256
        split = (trow + base >= length) & (tcol + base < length)
        ok = ((tcol < trow) & open_row & jnp.logical_not(split)) | (tcol == trow)
        s = jnp.where(ok, s, NEG)
        m = jnp.max(s, axis=1, keepdims=True)
        p = jnp.exp2(s - m)
        acc = jnp.dot(p.astype(BF), va[qi], preferred_element_type=F32)
        m_s[...] = m
        acc_s[...] = acc

        def step(ki, c2):
            s = lax.dot_general(qa[qi], ka[ki], nt, preferred_element_type=F32)
            m = m_s[...]
            m_new = jnp.maximum(m, jnp.max(s, axis=1, keepdims=True))
            p = jnp.exp2(s - m_new)
            acc_s[...] = acc_s[...] * jnp.exp2(m - m_new) + jnp.dot(
                p.astype(BF), va[ki], preferred_element_type=F32
            )
            m_s[...] = m_new
            return c2

        lax.fori_loop(0, qi, step, 0)
        acc = acc_s[...]
        out = acc / acc[:, 64:65]
        both = jnp.where(hlane < 64, out[:256], pltpu.roll(out[256:], 64, 1)).astype(BF)
        for half in range(2):
            j = 2 * qi + half
            tile[j] = both[half * TD : (half + 1) * TD]

            @pl.when(j != mp)
            def _():
                send(tile.at[j], att_in.at[mp], asend.at[j], arecv.at[mp], {"mp": j}).start()

            @pl.when(j == mp)
            def _():
                pltpu.make_async_copy(tile.at[j], att_in.at[j], lsem.at[1]).start()

        return carry

    lax.fori_loop(0, 4, block, 0)
    relay.stage2()
    lax.fori_loop(4, 5, block, 0)
    relay.stage1()
    lax.fori_loop(5, 7, block, 0)
    relay.stage3()
    lax.fori_loop(7, 8, block, 0)
    relay.stage4()
    relay.stage5()
    pltpu.make_async_copy(tile.at[mp], att_in.at[mp], lsem.at[1]).wait()
    for s in range(1, NMP):
        j = others[s - 1]
        copy = send(tile.at[j], att_in.at[j], asend.at[j], arecv.at[j], {"mp": j})
        copy.wait_send()
        copy.wait_recv()
    own_pages.wait()
    for s in range(1, NDP):
        started[s - 1].wait_send()
        i = lax.rem(dp + NDP - s, NDP)
        landed(cache.at[i], psend.at[s], precv.at[s], {"dp": i})
    relay.finish()


def run_attend(qkv, flags, kvrows, lens, table, wg, wu):
    sds = jax.ShapeDtypeStruct
    dma = pltpu.SemaphoreType.DMA
    return pl.pallas_call(
        attend,
        out_shape=(
            sds((NMP, TD, 128), BF),
            sds((NDP, 2, 16, 1024), BF),
            sds(wg.shape, BF),
            sds(wu.shape, BF),
        ),
        in_specs=[VM, VM, VM, SM, SM, ANY, ANY],
        out_specs=(ANY, ANY, ANY, ANY),
        input_output_aliases={5: 2, 6: 3},
        scratch_shapes=[
            pltpu.VMEM((8, 512, 128), BF),
            pltpu.VMEM((8, 256, 128), BF),
            pltpu.VMEM((8, 256, 128), BF),
            pltpu.VMEM((NMP, 8, TD), F32),
            pltpu.VMEM((NMP, TD, 128), BF),
            pltpu.VMEM((NDP, 2, 16, 1024), BF),
            pltpu.VMEM((512, 1), F32),
            pltpu.VMEM((512, 128), F32),
            dma((30,)), dma((16, 2)), dma((NMP,)), dma((NMP,)), dma((NDP,)), dma((NDP,)), dma((2,)),
        ],
        compiler_params=pltpu.CompilerParams(
            collective_id=2, has_side_effects=True, vmem_limit_bytes=VLIM
        ),
        name="attend",
    )(qkv, flags, kvrows, lens, table, wg, wu)


def mlp(
    att, tok, gain, wo, wg, wu, wd,
    out,
    att_v, wo_v, wg_v, wu_v, wd_v, hid, act, hbuf, part, rs, via,
    wsem, gs, gr, ss, sr, wss, wsr,
):
    dp, mp, chip, core = place()
    y, x = lax.div(chip, 2), lax.rem(chip, 2)
    yp, ym, y2, xo = lax.rem(y + 1, 4), lax.rem(y + 3, 4), lax.rem(y + 2, 4), 1 - x

    def dev(yy, xx):
        return {"mp": (yy * 2 + xx) * 2 + core}

    peers = [(y, xo), (yp, x), (ym, x), (yp, xo), (ym, xo), (y2, x), (y2, xo)]
    relay = Relay(lambda b, c, p: wd_v.at[b, c, pl.ds(p * 32, 32)], wss, wsr)
    barrier, count = greet([dev(*p) for p in peers] + [relay.partner, relay.up, relay.down, relay.across])
    loads = [
        pltpu.make_async_copy(wo, wo_v, wsem.at[0]),
        pltpu.make_async_copy(wg, wg_v, wsem.at[1]),
        pltpu.make_async_copy(wu, wu_v, wsem.at[2]),
        pltpu.make_async_copy(wd, wd_v.at[dp, core], wsem.at[3]),
    ]
    loads[3].start()
    for copy in loads[:3]:
        copy.start()
    pl.semaphore_wait(barrier, count)
    loads[3].wait()
    relay.stage0()
    for j in range(NMP):
        att_v[:, j * 128 : (j + 1) * 128] = att[j]
    loads[0].wait()

    def project(n, carry):
        cols = pl.ds(pl.multiple_of(n * 512, 512), 512)
        got = jnp.dot(att_v[...], wo_v[:, cols], preferred_element_type=F32)
        hid[:, cols] = (tok[:, cols].astype(F32) + got).astype(BF).astype(F32)
        return carry

    lax.fori_loop(0, 4, project, 0)
    act[chip] = norm_rows(hid[...], gain[...]).astype(BF)

    started = []
    half = (pl.ds(0, 64), pl.ds(64, 64))

    def forward(block, rows, event, to):
        ref = act.at[block] if rows is None else act.at[block, rows]
        copy = send(ref, ref, gs.at[len(started)], gr.at[event], dev(*to))
        copy.start()
        started.append(copy)

    def arrive(block, rows, event):
        ref = act.at[block] if rows is None else act.at[block, rows]
        landed(ref, gs.at[0], gr.at[event], dev(y, xo))

    def slot(yy, xx):
        return yy * 2 + xx

    mine = slot(y, x)
    forward(mine, None, 0, (y, xo))
    forward(mine, None, 1, (yp, x))
    forward(mine, None, 2, (ym, x))
    relay.stage2()
    relay.stage1()
    arrive(slot(y, xo), None, 0)
    forward(slot(y, xo), None, 3, (yp, x))
    forward(slot(y, xo), None, 4, (ym, x))
    arrive(slot(ym, x), None, 1)
    forward(slot(ym, x), half[0], 5, (yp, x))
    arrive(slot(yp, x), None, 2)
    forward(slot(yp, x), half[1], 6, (ym, x))
    relay.stage3()
    for copy in loads[1:3]:
        copy.wait()

    def widen(k, yy):
        rows = act.at[pl.ds(yy * 2, 2)]

        def hidden(n, carry):
            cols = pl.ds(pl.multiple_of(n * 256, 256), 256)
            xin = rows[...].reshape(256, D)
            g = jnp.dot(xin, wg_v[:, cols], preferred_element_type=F32)
            u = jnp.dot(xin, wu_v[:, cols], preferred_element_type=F32)
            hbuf[k, :, cols] = (g / (1.0 + jnp.exp(-g)) * u).astype(BF)
            return carry

        lax.fori_loop(0, 4, hidden, 0)

    def narrow(k, yy):
        def final(n, carry):
            cols = pl.ds(pl.multiple_of(n * 512, 512), 512)
            w = wd_v[:, :, :, cols].reshape(HB, 512)
            r = jnp.dot(hbuf[k], w, preferred_element_type=F32).astype(BF)
            part[yy * 2, :, cols] = r[:TD]
            part[yy * 2 + 1, :, cols] = r[TD:]
            return carry

        lax.fori_loop(0, 4, final, 0)

    sends = []

    def ship(src, dst, event, to):
        copy = send(src, dst, ss.at[event], sr.at[event], dev(*to))
        copy.start()
        sends.append(copy)

    def give(yy, xx, rows, event):
        ship(part.at[slot(yy, xx), rows], rs.at[mine, rows], event, (yy, xx))

    def taken(dst, event):
        landed(dst, ss.at[event], sr.at[event], dev(y, xo))

    widen(0, y)
    arrive(slot(ym, xo), None, 3)
    forward(slot(ym, xo), half[0], 7, (yp, x))
    arrive(slot(yp, xo), None, 4)
    forward(slot(yp, xo), half[1], 8, (ym, x))
    relay.stage4()
    widen(1, ym)
    widen(2, yp)
    relay.stage5()
    narrow(0, y)
    give(y, xo, pl.ds(0, TD), 0)
    narrow(1, ym)
    for k, xx in enumerate((x, xo)):
        give(ym, xx, half[0], 1 + k)
    narrow(2, yp)
    for k, xx in enumerate((x, xo)):
        give(yp, xx, half[1], 3 + k)
    arrive(slot(y2, x), half[0], 5)
    arrive(slot(y2, x), half[1], 6)
    arrive(slot(y2, xo), half[0], 7)
    arrive(slot(y2, xo), half[1], 8)
    widen(3, y2)
    narrow(3, y2)
    for k, xx in enumerate((xo, x)):
        ship(part.at[slot(y2, xx), half[0]], via.at[0, k], 5 + k, (yp, x))
        ship(part.at[slot(y2, xx), half[1]], via.at[1, k], 7 + k, (ym, x))
    for k, xx in enumerate((xo, x)):
        for side, (yy, event) in enumerate(((yp, 9), (ym, 11))):
            taken(via.at[side, k], 5 + 2 * side + k)
            ref = part.at[slot(yy, xx), half[side]]
            ref[...] = (ref[...].astype(F32) + via[side, k].astype(F32)).astype(BF)
            give(yy, xx, half[side], event + k)
    taken(rs.at[slot(y, xo)], 0)
    for k, xx in enumerate((x, xo)):
        taken(rs.at[slot(yp, xx), half[0]], 1 + k)
        taken(rs.at[slot(ym, xx), half[1]], 3 + k)
    for k, xx in enumerate((xo, x)):
        taken(rs.at[slot(ym, xx), half[0]], 9 + k)
        taken(rs.at[slot(yp, xx), half[1]], 11 + k)
    sources = [slot(y, xo), slot(ym, x), slot(ym, xo), slot(yp, x), slot(yp, xo)]

    def close(n, carry):
        cols = pl.ds(pl.multiple_of(n * 256, 256), 256)
        total = part[mine, :, cols].astype(F32)
        for c in sources:
            total = total + rs[c, :, cols].astype(F32)
        out[:, cols] = (hid[:, cols] + total).astype(BF)
        return carry

    lax.fori_loop(0, 8, close, 0)
    for copy in started + sends:
        copy.wait_send()
    relay.finish()


def run_mlp(att, tok, gain, wo, wg, wu, wd):
    dma = pltpu.SemaphoreType.DMA
    return pl.pallas_call(
        mlp,
        out_shape=jax.ShapeDtypeStruct((TD, D), BF),
        in_specs=[VM, VM, VM, ANY, ANY, ANY, ANY],
        out_specs=VM,
        scratch_shapes=[
            pltpu.VMEM((TD, D), BF),
            pltpu.VMEM((D, D), BF),
            pltpu.VMEM((D, HB), BF),
            pltpu.VMEM((D, HB), BF),
            pltpu.VMEM((8, 2, 64, D), BF),
            pltpu.VMEM((TD, D), F32),
            pltpu.VMEM((8, TD, D), BF),
            pltpu.VMEM((4, 256, HB), BF),
            pltpu.VMEM((8, TD, D), BF),
            pltpu.VMEM((8, TD, D), BF),
            pltpu.VMEM((2, 2, 64, D), BF),
            dma((4,)), dma((9,)), dma((9,)), dma((13,)), dma((13,)), dma((30,)), dma((16, 2)),
        ],
        compiler_params=pltpu.CompilerParams(
            collective_id=3, has_side_effects=True, vmem_limit_bytes=VLIM
        ),
        name="mlp",
    )(att, tok, gain, wo, wg, wu, wd)


def on_device(
    tokens, attn_gain, mlp_gain, query_weight, keyval_weight, output_weight,
    gate_rows, up_rows, down_rows, lengths, valid, page_table,
):
    qkv, flags, wg, wu, wd, kvrows = run_front(
        tokens, attn_gain.reshape(1, D), query_weight, keyval_weight,
        gate_rows, up_rows, down_rows, valid.reshape(1, TD),
    )
    att, cache, wg, wu = run_attend(qkv, flags, kvrows, lengths, page_table, wg, wu)
    layer_out = run_mlp(
        att, tokens, mlp_gain.reshape(1, D), output_weight,
        wg.reshape(D, HB), wu.reshape(D, HB), wd,
    )
    return (layer_out, cache[None, None])


def solution(mesh):
    return jax.shard_map(
        on_device,
        mesh=mesh,
        in_specs=(
            P(("dp", "mp"), None), P(), P(), P(), P(), P(),
            P(("dp", "mp"), None), P(("dp", "mp"), None), P(("dp", "mp"), None),
            P("dp", None), P(("dp", "mp")), P(("dp", "mp"), None),
        ),
        out_specs=(P(("dp", "mp"), None), P("dp", "mp", None, None, None, None)),
        check_vma=False,
    )
```

```python
import functools
import math

import jax
import jax.numpy as jnp
from jax import lax
from jax.experimental import pallas as pl
from jax.experimental.pallas import tpu as pltpu
from jax.sharding import PartitionSpec as P

MESH = pl.DeviceIdType.MESH
BF = jnp.bfloat16
F32 = jnp.float32
NDP = 8
NMP = 16
TD = 128
D = 2048
HB = 1024
NEG = -1e30
INNER = 16
ANY = pl.BlockSpec(memory_space=pl.ANY)
VM = pl.BlockSpec(memory_space=pltpu.VMEM)
SM = pl.BlockSpec(memory_space=pltpu.SMEM)
VLIM = 62 * 1024 * 1024


def place():
    dp = lax.axis_index("dp")
    mp = lax.axis_index("mp")
    return dp, mp, lax.div(mp, 2), lax.rem(mp, 2)


def greet(peers):
    barrier = pltpu.get_barrier_semaphore()
    for peer in peers:
        pl.semaphore_signal(barrier, inc=1, device_id=peer, device_id_type=MESH)
    return barrier, len(peers)


def send(src, dst, ssem, rsem, dev):
    copy = pltpu.make_async_remote_copy(
        src_ref=src, dst_ref=dst, send_sem=ssem, recv_sem=rsem, device_id=dev, device_id_type=MESH
    )
    return copy


def landed(dst, ssem, rsem, dev):
    send(dst, dst, ssem, rsem, dev).wait_recv()


def norm_rows(x, gain):
    ms = jnp.mean(x * x, axis=-1, keepdims=True)
    return x * lax.rsqrt(ms + 1e-05) * gain


def front(
    tok, gain, wq, wkv, gate, up, down, valid,
    qkv_in, flag_in, wg, wu, wd, kvrows,
    wv, normed, cs, sbuf, fbuf, gs, us, kbuf, vbuf,
    wsem, qs, qr, fs, fr, gsend, grecv, usend, urecv, lsem,
):
    dp, mp, chip, core = place()
    others = [lax.rem(mp + s, NMP) for s in range(1, NMP)]
    barrier, count = greet([{"mp": j} for j in others])
    wcopies = []
    for n in range(6):
        src = wkv.at[:, pl.ds((n - 4) * 512, 512)] if n >= 4 else wq.at[:, pl.ds(n * 512, 512)]
        wcopies.append(pltpu.make_async_copy(src, wv.at[n], wsem.at[n]))
    order = (4, 5, 0, 1, 2, 3)
    for n in order:
        wcopies[n].start()
    for c in range(8):
        for i in range(8):
            cols = slice((i * 8 + c) * 128, (i * 8 + c + 1) * 128)
            gs[c, :, i * 128 : (i + 1) * 128] = gate[:, cols].astype(BF)
            us[c, :, i * 128 : (i + 1) * 128] = up[:, cols].astype(BF)
    wd[...] = down[...].astype(BF)
    fbuf[...] = jnp.broadcast_to(valid[...].astype(F32), (16, TD)).astype(BF)
    local = [
        pltpu.make_async_copy(gs.at[chip], wg.at[dp, chip, core], lsem.at[0]),
        pltpu.make_async_copy(us.at[chip], wu.at[dp, chip, core], lsem.at[1]),
        pltpu.make_async_copy(fbuf, flag_in.at[mp], lsem.at[2]),
    ]
    for copy in local:
        copy.start()
    pl.semaphore_wait(barrier, count)
    started = []
    for s in range(1, 8):
        c = lax.rem(chip + s, 8)
        dev = {"mp": c * 2 + core}
        for buf, out, ss, rs in ((gs, wg, gsend, grecv), (us, wu, usend, urecv)):
            copy = send(buf.at[c], out.at[dp, chip, core], ss.at[s], rs.at[s], dev)
            copy.start()
            started.append(copy)
    for s in range(1, NMP):
        copy = send(fbuf, flag_in.at[mp], fs.at[s], fr.at[s], {"mp": others[s - 1]})
        copy.start()
        started.append(copy)

    x = tok[...].astype(F32)
    normed[...] = norm_rows(x, gain[...]).astype(BF)
    lane = lax.broadcasted_iota(jnp.int32, (TD, 128), 1)
    row = lax.broadcasted_iota(jnp.int32, (TD, 128), 0) + mp * TD
    pos = row.astype(F32)
    freq = jnp.exp(lax.rem(lane, 32).astype(F32) * (-(2.0 / 64.0) * math.log(500000.0)))
    angle = pos * freq
    cs[0] = jnp.cos(angle)
    cs[1] = jnp.sin(angle)
    low = lane < 64
    first = lax.rem(lane, 64) < 32

    def turn(t):
        after = pltpu.roll(t, 96, 1)
        before = pltpu.roll(t, 32, 1)
        return t * cs[0] + jnp.where(first, -after, before) * cs[1]

    for n in order:
        wcopies[n].wait()
        acc = jnp.dot(normed[...], wv[n], preferred_element_type=F32)
        for l in range(4):
            t = acc[:, l * 128 : (l + 1) * 128]
            if n == 4:
                t = turn(t)
                kbuf[:, l * 128 : (l + 1) * 128] = t
                kvrows[:, l * 128 : (l + 1) * 128] = t.astype(BF)
            elif n == 5:
                vbuf[:, l * 128 : (l + 1) * 128] = t
                kvrows[:, 512 + l * 128 : 512 + (l + 1) * 128] = t.astype(BF)
            else:
                sbuf[n * 4 + l, 0] = (turn(t) * (0.125 * math.log2(math.e))).astype(BF)
        if n == 5:
            for l in range(4):
                kt = kbuf[:, l * 128 : (l + 1) * 128]
                vt = vbuf[:, l * 128 : (l + 1) * 128]
                even = jnp.where(low, kt, pltpu.roll(vt, 64, 1)).astype(BF)
                odd = jnp.where(low, pltpu.roll(kt, 64, 1), vt).astype(BF)
                sbuf[4 * l, 1] = even
                sbuf[4 * l + 1, 1] = even
                sbuf[4 * l + 2, 1] = odd
                sbuf[4 * l + 3, 1] = odd
    own = pltpu.make_async_copy(sbuf.at[mp], qkv_in.at[mp], lsem.at[3])
    own.start()
    for s in range(1, NMP):
        j = others[s - 1]
        copy = send(sbuf.at[j], qkv_in.at[mp], qs.at[s], qr.at[s], {"mp": j})
        copy.start()
        started.append(copy)
    own.wait()
    for copy in local:
        copy.wait()
    for copy in started:
        copy.wait_send()
    for s in range(1, 8):
        c = lax.rem(chip + 8 - s, 8)
        dev = {"mp": c * 2 + core}
        landed(wg.at[dp, c, core], gsend.at[s], grecv.at[s], dev)
        landed(wu.at[dp, c, core], usend.at[s], urecv.at[s], dev)
    for s in range(1, NMP):
        j = lax.rem(mp + NMP - s, NMP)
        landed(flag_in.at[j], fs.at[s], fr.at[s], {"mp": j})
        landed(qkv_in.at[j], qs.at[s], qr.at[s], {"mp": j})


def run_front(tok, gain, wq, wkv, gate, up, down, valid):
    sds = jax.ShapeDtypeStruct
    dma = pltpu.SemaphoreType.DMA
    return pl.pallas_call(
        front,
        out_shape=(
            sds((NMP, 2, TD, 128), BF),
            sds((NMP, 16, TD), BF),
            sds((8, 8, 2, 16, HB), BF),
            sds((8, 8, 2, 16, HB), BF),
            sds((64, D), BF),
            sds((TD, 1024), BF),
        ),
        in_specs=[VM, VM, ANY, ANY, VM, VM, VM, VM],
        out_specs=(ANY, ANY, ANY, ANY, VM, VM),
        scratch_shapes=[
            pltpu.VMEM((6, D, 512), BF),
            pltpu.VMEM((TD, D), BF),
            pltpu.VMEM((2, TD, 128), F32),
            pltpu.VMEM((NMP, 2, TD, 128), BF),
            pltpu.VMEM((16, TD), BF),
            pltpu.VMEM((8, 16, HB), BF),
            pltpu.VMEM((8, 16, HB), BF),
            pltpu.VMEM((TD, 512), F32),
            pltpu.VMEM((TD, 512), F32),
            dma((6,)), dma((NMP,)), dma((NMP,)), dma((NMP,)), dma((NMP,)),
            dma((8,)), dma((8,)), dma((8,)), dma((8,)), dma((4,)),
        ],
        compiler_params=pltpu.CompilerParams(
            collective_id=1, has_side_effects=True, vmem_limit_bytes=VLIM
        ),
        name="front",
    )(tok, gain, wq, wkv, gate, up, down, valid)


class Relay:
    def __init__(self, part, ssem, rsem):
        self.part, self.ssem, self.rsem = part, ssem, rsem
        dp, mp, chip, core = place()
        z, xh = lax.div(dp, 2), lax.rem(dp, 2)
        self.core, self.xh = core, xh
        self.zm, self.zp, self.z2, self.z = lax.rem(z + 3, 4), lax.rem(z + 1, 4), lax.rem(z + 2, 4), z
        self.xo = 1 - xh
        self.partner = {"mp": chip * 2 + 1 - core}
        self.up = {"dp": self.zp * 2 + xh}
        self.down = {"dp": self.zm * 2 + xh}
        self.across = {"dp": z * 2 + self.xo}
        self.count = 0
        self.started = []

    def put(self, block, parts, event, dev):
        for p in parts:
            ref = self.part(block, self.core, p)
            copy = send(ref, ref, self.ssem.at[self.count], self.rsem.at[event, p], dev)
            copy.start()
            self.started.append(copy)
            self.count += 1

    def got(self, block, parts, event, core=None):
        for p in parts:
            ref = self.part(block, self.core if core is None else core, p)
            landed(ref, self.ssem.at[0], self.rsem.at[event, p], self.partner)

    def finish(self):
        for copy in self.started:
            copy.wait_send()

    def stage0(self):
        b = self.z * 2 + self.xh
        self.put(b, (0, 1), 0, self.across)
        self.put(b, (0, 1), 1, self.up)
        self.put(b, (0, 1), 2, self.down)
        self.put(b, (0, 1), 8, self.partner)

    def stage1(self):
        b = self.z * 2 + self.xo
        self.got(b, (0, 1), 0)
        self.put(b, (0, 1), 3, self.up)
        self.put(b, (0, 1), 4, self.down)
        self.put(b, (0, 1), 9, self.partner)

    def stage2(self):
        b = self.zm * 2 + self.xh
        self.got(b, (0, 1), 1)
        self.put(b, (0,), 5, self.up)
        self.put(b, (0, 1), 10, self.partner)
        b = self.zp * 2 + self.xh
        self.got(b, (0, 1), 2)
        self.put(b, (1,), 5, self.down)
        self.put(b, (0, 1), 11, self.partner)

    def stage3(self):
        b = self.zm * 2 + self.xo
        self.got(b, (0, 1), 3)
        self.put(b, (0,), 6, self.up)
        self.put(b, (0, 1), 12, self.partner)
        b = self.zp * 2 + self.xo
        self.got(b, (0, 1), 4)
        self.put(b, (1,), 6, self.down)
        self.put(b, (0, 1), 13, self.partner)

    def stage4(self):
        b = self.z2 * 2 + self.xh
        self.got(b, (0, 1), 5)
        self.put(b, (0, 1), 14, self.partner)
        b = self.z2 * 2 + self.xo
        self.got(b, (0, 1), 6)
        self.put(b, (0, 1), 15, self.partner)

    def stage5(self):
        blocks = (
            self.z * 2 + self.xh, self.z * 2 + self.xo, self.zm * 2 + self.xh, self.zp * 2 + self.xh,
            self.zm * 2 + self.xo, self.zp * 2 + self.xo, self.z2 * 2 + self.xh, self.z2 * 2 + self.xo,
        )
        for e, b in enumerate(blocks):
            self.got(b, (0, 1), 8 + e, 1 - self.core)


def attend(
    qkv, flags, kvrows, lens, table, wg_i, wu_i,
    att_in, cache, wg, wu,
    qa, ka, va, fb, tile, pbuf, m_s, acc_s,
    ssem, rsem, asend, arecv, psend, precv, lsem,
):
    dp, mp, chip, core = place()
    others = [lax.rem(mp + s, NMP) for s in range(1, NMP)]
    dothers = [lax.rem(dp + s, NDP) for s in range(1, NDP)]
    barrier, count = greet([{"mp": j} for j in others] + [{"dp": i} for i in dothers])
    relay = Relay(lambda b, c, p: (wg, wu)[p].at[b, :, c], ssem, rsem)
    length = lens[0, 0]

    holder = [table[p, 0] for p in range(8)]
    target = []
    for p in range(8):
        rank = jnp.int32(0)
        for q in range(p):
            rank = rank + jnp.where(holder[q] == holder[p], 1, 0)
        target.append(holder[p] * 2 + rank)
    col = lax.broadcasted_iota(jnp.int32, (256, 128), 1)
    row = lax.broadcasted_iota(jnp.int32, (256, 128), 0)
    want = jnp.zeros((256, 128), jnp.int32)
    for p in range(8):
        want = jnp.where(lax.div(col, 16) == p, target[p], want)
    pick = (lax.div(row, 16) == want) & (lax.rem(row, 16) == lax.rem(col, 16))
    pick = jnp.where(pick, 1.0, 0.0).astype(BF)
    pages = jnp.dot(pick, kvrows[...], preferred_element_type=F32).astype(BF)
    for i in range(8):
        for r in range(2):
            pbuf[i, r] = pages[(i * 2 + r) * 16 : (i * 2 + r + 1) * 16]

    pl.semaphore_wait(barrier, count)
    relay.stage0()
    started = []
    own_pages = pltpu.make_async_copy(pbuf.at[dp], cache.at[dp], lsem.at[0])
    own_pages.start()
    for s in range(1, NDP):
        i = dothers[s - 1]
        copy = send(pbuf.at[i], cache.at[dp], psend.at[s], precv.at[s], {"dp": i})
        copy.start()
        started.append(copy)

    lane = lax.broadcasted_iota(jnp.int32, (TD, 128), 1)
    sub = lax.broadcasted_iota(jnp.int32, (TD, 128), 0)
    low = lane < 64

    def prepare(b, carry):
        q = qkv[b, 0].astype(F32)
        kv = qkv[b, 1].astype(F32)
        frow = flags[b].astype(F32)[0:1, :]
        token = sub + b * TD
        late = jnp.where(token >= length, 1.0, 0.0)
        extra = jnp.where(lane == 64, 1.0, jnp.where(lane == 65, late, 0.0))
        qi, half = lax.div(b, 2), lax.rem(b, 2)
        qa[qi, pl.ds(half * TD, TD), :] = jnp.where(low, q, extra).astype(BF)
        qa[qi, pl.ds(256 + half * TD, TD), :] = jnp.where(low, pltpu.roll(q, 64, 1), extra).astype(BF)
        fcol = jnp.sum(jnp.where(lane == sub, frow, 0.0), axis=1, keepdims=True)
        closed = jnp.where(fcol > 0.5, 0.0, NEG)
        early = jnp.where(token >= length, 0.0, NEG)
        bias = jnp.where(lane == 64, closed, jnp.where(lane == 65, early, 0.0))
        ka[qi, pl.ds(half * TD, TD), :] = jnp.where(low, kv, bias).astype(BF)
        one = jnp.where(lane == 64, 1.0, 0.0)
        va[qi, pl.ds(half * TD, TD), :] = jnp.where(low, pltpu.roll(kv, 64, 1), one).astype(BF)
        fb[b] = jnp.broadcast_to(frow, (8, TD))
        return carry

    lax.fori_loop(0, NMP, prepare, 0)

    trow = lax.broadcasted_iota(jnp.int32, (512, 256), 0)
    trow = lax.rem(trow, 256)
    tcol = lax.broadcasted_iota(jnp.int32, (512, 256), 1)
    nt = (((1,), (1,)), ((), ()))
    qlane = lax.broadcasted_iota(jnp.int32, (512, 128), 1)
    hlane = lax.broadcasted_iota(jnp.int32, (256, 128), 1)

    def block(qi, carry):
        q = qa[qi]
        bare = jnp.where(qlane < 64, q.astype(F32), 0.0).astype(BF)
        s = lax.dot_general(bare, ka[qi], nt, preferred_element_type=F32)
        open_row = jnp.concatenate([fb[2 * qi][0:1], fb[2 * qi + 1][0:1]], axis=1) > 0.5
        base = qi * 256
        split = (trow + base >= length) & (tcol + base < length)
        ok = ((tcol < trow) & open_row & jnp.logical_not(split)) | (tcol == trow)
        s = jnp.where(ok, s, NEG)
        m = jnp.max(s, axis=1, keepdims=True)
        p = jnp.exp2(s - m)
        acc = jnp.dot(p.astype(BF), va[qi], preferred_element_type=F32)
        m_s[...] = m
        acc_s[...] = acc

        def step(ki, c2):
            s = lax.dot_general(qa[qi], ka[ki], nt, preferred_element_type=F32)
            m = m_s[...]
            m_new = jnp.maximum(m, jnp.max(s, axis=1, keepdims=True))
            p = jnp.exp2(s - m_new)
            acc_s[...] = acc_s[...] * jnp.exp2(m - m_new) + jnp.dot(
                p.astype(BF), va[ki], preferred_element_type=F32
            )
            m_s[...] = m_new
            return c2

        lax.fori_loop(0, qi, step, 0)
        acc = acc_s[...]
        out = acc / acc[:, 64:65]
        both = jnp.where(hlane < 64, out[:256], pltpu.roll(out[256:], 64, 1)).astype(BF)
        for half in range(2):
            j = 2 * qi + half
            tile[j] = both[half * TD : (half + 1) * TD]

            @pl.when(j != mp)
            def _():
                send(tile.at[j], att_in.at[mp], asend.at[j], arecv.at[mp], {"mp": j}).start()

            @pl.when(j == mp)
            def _():
                pltpu.make_async_copy(tile.at[j], att_in.at[j], lsem.at[1]).start()

        return carry

    lax.fori_loop(0, 4, block, 0)
    relay.stage2()
    lax.fori_loop(4, 5, block, 0)
    relay.stage1()
    lax.fori_loop(5, 7, block, 0)
    relay.stage3()
    lax.fori_loop(7, 8, block, 0)
    relay.stage4()
    relay.stage5()
    pltpu.make_async_copy(tile.at[mp], att_in.at[mp], lsem.at[1]).wait()
    for s in range(1, NMP):
        j = others[s - 1]
        copy = send(tile.at[j], att_in.at[j], asend.at[j], arecv.at[j], {"mp": j})
        copy.wait_send()
        copy.wait_recv()
    own_pages.wait()
    for s in range(1, NDP):
        started[s - 1].wait_send()
        i = lax.rem(dp + NDP - s, NDP)
        landed(cache.at[i], psend.at[s], precv.at[s], {"dp": i})
    relay.finish()


def run_attend(qkv, flags, kvrows, lens, table, wg, wu):
    sds = jax.ShapeDtypeStruct
    dma = pltpu.SemaphoreType.DMA
    return pl.pallas_call(
        attend,
        out_shape=(
            sds((NMP, TD, 128), BF),
            sds((NDP, 2, 16, 1024), BF),
            sds(wg.shape, BF),
            sds(wu.shape, BF),
        ),
        in_specs=[VM, VM, VM, SM, SM, ANY, ANY],
        out_specs=(ANY, ANY, ANY, ANY),
        input_output_aliases={5: 2, 6: 3},
        scratch_shapes=[
            pltpu.VMEM((8, 512, 128), BF),
            pltpu.VMEM((8, 256, 128), BF),
            pltpu.VMEM((8, 256, 128), BF),
            pltpu.VMEM((NMP, 8, TD), F32),
            pltpu.VMEM((NMP, TD, 128), BF),
            pltpu.VMEM((NDP, 2, 16, 1024), BF),
            pltpu.VMEM((512, 1), F32),
            pltpu.VMEM((512, 128), F32),
            dma((30,)), dma((16, 2)), dma((NMP,)), dma((NMP,)), dma((NDP,)), dma((NDP,)), dma((2,)),
        ],
        compiler_params=pltpu.CompilerParams(
            collective_id=2, has_side_effects=True, vmem_limit_bytes=VLIM
        ),
        name="attend",
    )(qkv, flags, kvrows, lens, table, wg, wu)


def mlp(
    att, tok, gain, wo, wg, wu, wd,
    out,
    att_v, wo_v, wg_v, wu_v, wd_v, hid, act, hbuf, part, rs, via,
    wsem, gs, gr, ss, sr, wss, wsr,
):
    dp, mp, chip, core = place()
    y, x = lax.div(chip, 2), lax.rem(chip, 2)
    yp, ym, y2, xo = lax.rem(y + 1, 4), lax.rem(y + 3, 4), lax.rem(y + 2, 4), 1 - x

    def dev(yy, xx):
        return {"mp": (yy * 2 + xx) * 2 + core}

    peers = [(y, xo), (yp, x), (ym, x), (yp, xo), (ym, xo), (y2, x), (y2, xo)]
    relay = Relay(lambda b, c, p: wd_v.at[b, c, pl.ds(p * 32, 32)], wss, wsr)
    barrier, count = greet([dev(*p) for p in peers] + [relay.partner, relay.up, relay.down, relay.across])
    loads = [
        pltpu.make_async_copy(wg, wg_v, wsem.at[0]),
        pltpu.make_async_copy(wu, wu_v, wsem.at[1]),
        pltpu.make_async_copy(wd, wd_v.at[dp, core], wsem.at[2]),
    ]
    wo_loads = [
        pltpu.make_async_copy(wo.at[:, pl.ds(n * 512, 512)], wo_v.at[n], wsem.at[3 + n]) for n in range(4)
    ]
    loads[2].start()
    for copy in wo_loads:
        copy.start()
    pl.semaphore_wait(barrier, count)
    loads[2].wait()
    relay.stage0()
    for j in range(NMP):
        att_v[:, j * 128 : (j + 1) * 128] = att[j]
    for n in range(4):
        cols = slice(n * 512, (n + 1) * 512)
        wo_loads[n].wait()
        got = jnp.dot(att_v[...], wo_v[n], preferred_element_type=F32)
        hid[:, cols] = (tok[:, cols].astype(F32) + got).astype(BF).astype(F32)
    for copy in loads[:2]:
        copy.start()
    act[chip] = norm_rows(hid[...], gain[...]).astype(BF)

    started = []
    half = (pl.ds(0, 64), pl.ds(64, 64))
    inner = (pl.ds(64 - INNER, INNER), pl.ds(64, INNER))
    both = pl.ds(64 - INNER, 2 * INNER)
    outer = (pl.ds(0, 64 - INNER), pl.ds(64 + INNER, 64 - INNER))

    def forward(block, rows, event, to):
        ref = act.at[block] if rows is None else act.at[block, rows]
        copy = send(ref, ref, gs.at[len(started)], gr.at[event], dev(*to))
        copy.start()
        started.append(copy)

    def arrive(block, rows, event):
        ref = act.at[block] if rows is None else act.at[block, rows]
        landed(ref, gs.at[0], gr.at[event], dev(y, xo))

    def slot(yy, xx):
        return yy * 2 + xx

    mine = slot(y, x)
    forward(mine, None, 0, (y, xo))
    forward(mine, None, 1, (yp, x))
    forward(mine, None, 2, (ym, x))
    relay.stage2()
    relay.stage1()
    arrive(slot(y, xo), None, 0)
    for i in range(2):
        forward(slot(y, xo), outer[i], 3 + i, (yp, x))
        forward(slot(y, xo), outer[i], 5 + i, (ym, x))
    arrive(slot(ym, x), None, 1)
    forward(slot(ym, x), half[0], 7, (yp, x))
    forward(slot(ym, x), both, 9, (y, xo))
    arrive(slot(yp, x), None, 2)
    forward(slot(yp, x), half[1], 8, (ym, x))
    forward(slot(yp, x), both, 10, (y, xo))
    relay.stage3()
    for copy in loads[:2]:
        copy.wait()

    def widen(k, yy):
        rows = act.at[pl.ds(yy * 2, 2)]

        def hidden(n, carry):
            cols = pl.ds(pl.multiple_of(n * 256, 256), 256)
            xin = rows[...].reshape(256, D)
            g = jnp.dot(xin, wg_v[:, cols], preferred_element_type=F32)
            u = jnp.dot(xin, wu_v[:, cols], preferred_element_type=F32)
            hbuf[k, :, cols] = (g / (1.0 + jnp.exp(-g)) * u).astype(BF)
            return carry

        lax.fori_loop(0, 4, hidden, 0)

    def narrow(k, yy):
        def final(n, carry):
            cols = pl.ds(pl.multiple_of(n * 512, 512), 512)
            w = wd_v[:, :, :, cols].reshape(HB, 512)
            r = jnp.dot(hbuf[k], w, preferred_element_type=F32).astype(BF)
            part[yy * 2, :, cols] = r[:TD]
            part[yy * 2 + 1, :, cols] = r[TD:]
            return carry

        lax.fori_loop(0, 4, final, 0)

    sends = []

    def ship(src, dst, event, to):
        copy = send(src, dst, ss.at[event], sr.at[event], dev(*to))
        copy.start()
        sends.append(copy)

    def give(yy, xx, rows, event):
        ship(part.at[slot(yy, xx), rows], rs.at[mine, rows], event, (yy, xx))

    def taken(dst, event):
        landed(dst, ss.at[event], sr.at[event], dev(y, xo))

    widen(0, y)
    arrive(slot(ym, xo), outer[0], 3)
    forward(slot(ym, xo), outer[0], 11, (yp, x))
    arrive(slot(yp, xo), outer[1], 6)
    forward(slot(yp, xo), outer[1], 12, (ym, x))
    relay.stage4()
    arrive(slot(ym, xo), outer[1], 4)
    arrive(slot(ym, xo), both, 9)
    widen(1, ym)
    arrive(slot(y2, x), half[0], 7)
    forward(slot(y2, x), inner[0], 13, (y, xo))
    arrive(slot(y2, x), half[1], 8)
    forward(slot(y2, x), inner[1], 14, (y, xo))
    arrive(slot(yp, xo), outer[0], 5)
    arrive(slot(yp, xo), both, 10)
    widen(2, yp)
    relay.stage5()
    narrow(0, y)
    give(y, xo, pl.ds(0, TD), 0)
    narrow(1, ym)
    for k, xx in enumerate((x, xo)):
        give(ym, xx, half[0], 1 + k)
    narrow(2, yp)
    for k, xx in enumerate((x, xo)):
        give(yp, xx, half[1], 3 + k)
    for i in range(2):
        arrive(slot(y2, xo), outer[i], 11 + i)
        arrive(slot(y2, xo), inner[i], 13 + i)
    widen(3, y2)
    narrow(3, y2)
    for k, xx in enumerate((xo, x)):
        ship(part.at[slot(y2, xx), half[0]], via.at[0, k], 5 + k, (yp, x))
        ship(part.at[slot(y2, xx), half[1]], via.at[1, k], 7 + k, (ym, x))
    for k, xx in enumerate((xo, x)):
        for side, (yy, event) in enumerate(((yp, 9), (ym, 11))):
            taken(via.at[side, k], 5 + 2 * side + k)
            ref = part.at[slot(yy, xx), half[side]]
            ref[...] = (ref[...].astype(F32) + via[side, k].astype(F32)).astype(BF)
            give(yy, xx, half[side], event + k)
    taken(rs.at[slot(y, xo)], 0)
    for k, xx in enumerate((x, xo)):
        taken(rs.at[slot(yp, xx), half[0]], 1 + k)
        taken(rs.at[slot(ym, xx), half[1]], 3 + k)
    for k, xx in enumerate((xo, x)):
        taken(rs.at[slot(ym, xx), half[0]], 9 + k)
        taken(rs.at[slot(yp, xx), half[1]], 11 + k)
    sources = [slot(y, xo), slot(ym, x), slot(ym, xo), slot(yp, x), slot(yp, xo)]

    def close(n, carry):
        cols = pl.ds(pl.multiple_of(n * 256, 256), 256)
        total = part[mine, :, cols].astype(F32)
        for c in sources:
            total = total + rs[c, :, cols].astype(F32)
        out[:, cols] = (hid[:, cols] + total).astype(BF)
        return carry

    lax.fori_loop(0, 8, close, 0)
    for copy in started + sends:
        copy.wait_send()
    relay.finish()


def run_mlp(att, tok, gain, wo, wg, wu, wd):
    dma = pltpu.SemaphoreType.DMA
    return pl.pallas_call(
        mlp,
        out_shape=jax.ShapeDtypeStruct((TD, D), BF),
        in_specs=[VM, VM, VM, ANY, ANY, ANY, ANY],
        out_specs=VM,
        scratch_shapes=[
            pltpu.VMEM((TD, D), BF),
            pltpu.VMEM((4, D, 512), BF),
            pltpu.VMEM((D, HB), BF),
            pltpu.VMEM((D, HB), BF),
            pltpu.VMEM((8, 2, 64, D), BF),
            pltpu.VMEM((TD, D), F32),
            pltpu.VMEM((8, TD, D), BF),
            pltpu.VMEM((4, 256, HB), BF),
            pltpu.VMEM((8, TD, D), BF),
            pltpu.VMEM((8, TD, D), BF),
            pltpu.VMEM((2, 2, 64, D), BF),
            dma((7,)), dma((15,)), dma((15,)), dma((13,)), dma((13,)), dma((30,)), dma((16, 2)),
        ],
        compiler_params=pltpu.CompilerParams(
            collective_id=3, has_side_effects=True, vmem_limit_bytes=VLIM
        ),
        name="mlp",
    )(att, tok, gain, wo, wg, wu, wd)


def on_device(
    tokens, attn_gain, mlp_gain, query_weight, keyval_weight, output_weight,
    gate_rows, up_rows, down_rows, lengths, valid, page_table,
):
    qkv, flags, wg, wu, wd, kvrows = run_front(
        tokens, attn_gain.reshape(1, D), query_weight, keyval_weight,
        gate_rows, up_rows, down_rows, valid.reshape(1, TD),
    )
    att, cache, wg, wu = run_attend(qkv, flags, kvrows, lengths, page_table, wg, wu)
    layer_out = run_mlp(
        att, tokens, mlp_gain.reshape(1, D), output_weight,
        wg.reshape(D, HB), wu.reshape(D, HB), wd,
    )
    return (layer_out, cache[None, None])


def solution(mesh):
    return jax.shard_map(
        on_device,
        mesh=mesh,
        in_specs=(
            P(("dp", "mp"), None), P(), P(), P(), P(), P(),
            P(("dp", "mp"), None), P(("dp", "mp"), None), P(("dp", "mp"), None),
            P("dp", None), P(("dp", "mp")), P(("dp", "mp"), None),
        ),
        out_specs=(P(("dp", "mp"), None), P("dp", "mp", None, None, None, None)),
        check_vma=False,
    )
```

```python
import functools
import math

import jax
import jax.numpy as jnp
from jax import lax
from jax.experimental import pallas as pl
from jax.experimental.pallas import tpu as pltpu
from jax.sharding import PartitionSpec as P

MESH = pl.DeviceIdType.MESH
BF = jnp.bfloat16
F32 = jnp.float32
NDP = 8
NMP = 16
TD = 128
D = 2048
HB = 1024
NEG = -1e30
INNER = 16
ANY = pl.BlockSpec(memory_space=pl.ANY)
VM = pl.BlockSpec(memory_space=pltpu.VMEM)
SM = pl.BlockSpec(memory_space=pltpu.SMEM)
VLIM = 62 * 1024 * 1024


def place():
    dp = lax.axis_index("dp")
    mp = lax.axis_index("mp")
    return dp, mp, lax.div(mp, 2), lax.rem(mp, 2)


def greet(peers):
    barrier = pltpu.get_barrier_semaphore()
    for peer in peers:
        pl.semaphore_signal(barrier, inc=1, device_id=peer, device_id_type=MESH)
    return barrier, len(peers)


def send(src, dst, ssem, rsem, dev):
    copy = pltpu.make_async_remote_copy(
        src_ref=src, dst_ref=dst, send_sem=ssem, recv_sem=rsem, device_id=dev, device_id_type=MESH
    )
    return copy


def landed(dst, ssem, rsem, dev):
    send(dst, dst, ssem, rsem, dev).wait_recv()


def norm_rows(x, gain):
    ms = jnp.mean(x * x, axis=-1, keepdims=True)
    return x * lax.rsqrt(ms + 1e-05) * gain


def front(
    tok, gain, wq, wkv, gate, up, down, valid,
    qkv_in, flag_in, wg, wu, wd, kvrows,
    wv, normed, cs, sbuf, fbuf, gs, us, kbuf, vbuf,
    wsem, qs, qr, fs, fr, gsend, grecv, usend, urecv, lsem,
):
    dp, mp, chip, core = place()
    others = [lax.rem(mp + s, NMP) for s in range(1, NMP)]
    barrier, count = greet([{"mp": j} for j in others])
    wcopies = []
    for n in range(6):
        src = wkv.at[:, pl.ds((n - 4) * 512, 512)] if n >= 4 else wq.at[:, pl.ds(n * 512, 512)]
        wcopies.append(pltpu.make_async_copy(src, wv.at[n], wsem.at[n]))
    order = (4, 5, 0, 1, 2, 3)
    for n in order:
        wcopies[n].start()
    for c in range(8):
        for i in range(8):
            cols = slice((i * 8 + c) * 128, (i * 8 + c + 1) * 128)
            gs[c, :, i * 128 : (i + 1) * 128] = gate[:, cols].astype(BF)
            us[c, :, i * 128 : (i + 1) * 128] = up[:, cols].astype(BF)
    wd[...] = down[...].astype(BF)
    fbuf[...] = jnp.broadcast_to(valid[...].astype(F32), (16, TD)).astype(BF)
    local = [
        pltpu.make_async_copy(gs.at[chip], wg.at[dp, chip, core], lsem.at[0]),
        pltpu.make_async_copy(us.at[chip], wu.at[dp, chip, core], lsem.at[1]),
        pltpu.make_async_copy(fbuf, flag_in.at[mp], lsem.at[2]),
    ]
    for copy in local:
        copy.start()
    pl.semaphore_wait(barrier, count)
    started = []
    for s in range(1, 8):
        c = lax.rem(chip + s, 8)
        dev = {"mp": c * 2 + core}
        for buf, out, ss, rs in ((gs, wg, gsend, grecv), (us, wu, usend, urecv)):
            copy = send(buf.at[c], out.at[dp, chip, core], ss.at[s], rs.at[s], dev)
            copy.start()
            started.append(copy)
    for s in range(1, NMP):
        copy = send(fbuf, flag_in.at[mp], fs.at[s], fr.at[s], {"mp": others[s - 1]})
        copy.start()
        started.append(copy)

    x = tok[...].astype(F32)
    normed[...] = norm_rows(x, gain[...]).astype(BF)
    lane = lax.broadcasted_iota(jnp.int32, (TD, 128), 1)
    row = lax.broadcasted_iota(jnp.int32, (TD, 128), 0) + mp * TD
    pos = row.astype(F32)
    freq = jnp.exp(lax.rem(lane, 32).astype(F32) * (-(2.0 / 64.0) * math.log(500000.0)))
    angle = pos * freq
    cs[0] = jnp.cos(angle)
    cs[1] = jnp.sin(angle)
    low = lane < 64
    first = lax.rem(lane, 64) < 32

    def turn(t):
        after = pltpu.roll(t, 96, 1)
        before = pltpu.roll(t, 32, 1)
        return t * cs[0] + jnp.where(first, -after, before) * cs[1]

    for n in order:
        wcopies[n].wait()
        acc = jnp.dot(normed[...], wv[n], preferred_element_type=F32)
        for l in range(4):
            t = acc[:, l * 128 : (l + 1) * 128]
            if n == 4:
                t = turn(t)
                kbuf[:, l * 128 : (l + 1) * 128] = t
                kvrows[:, l * 128 : (l + 1) * 128] = t.astype(BF)
            elif n == 5:
                vbuf[:, l * 128 : (l + 1) * 128] = t
                kvrows[:, 512 + l * 128 : 512 + (l + 1) * 128] = t.astype(BF)
            else:
                sbuf[n * 4 + l, 0] = (turn(t) * (0.125 * math.log2(math.e))).astype(BF)
        if n == 5:
            for l in range(4):
                kt = kbuf[:, l * 128 : (l + 1) * 128]
                vt = vbuf[:, l * 128 : (l + 1) * 128]
                even = jnp.where(low, kt, pltpu.roll(vt, 64, 1)).astype(BF)
                odd = jnp.where(low, pltpu.roll(kt, 64, 1), vt).astype(BF)
                sbuf[4 * l, 1] = even
                sbuf[4 * l + 1, 1] = even
                sbuf[4 * l + 2, 1] = odd
                sbuf[4 * l + 3, 1] = odd
    own = pltpu.make_async_copy(sbuf.at[mp], qkv_in.at[mp], lsem.at[3])
    own.start()
    for s in range(1, NMP):
        j = others[s - 1]
        copy = send(sbuf.at[j], qkv_in.at[mp], qs.at[s], qr.at[s], {"mp": j})
        copy.start()
        started.append(copy)
    own.wait()
    for copy in local:
        copy.wait()
    for copy in started:
        copy.wait_send()
    for s in range(1, 8):
        c = lax.rem(chip + 8 - s, 8)
        dev = {"mp": c * 2 + core}
        landed(wg.at[dp, c, core], gsend.at[s], grecv.at[s], dev)
        landed(wu.at[dp, c, core], usend.at[s], urecv.at[s], dev)
    for s in range(1, NMP):
        j = lax.rem(mp + NMP - s, NMP)
        landed(flag_in.at[j], fs.at[s], fr.at[s], {"mp": j})
        landed(qkv_in.at[j], qs.at[s], qr.at[s], {"mp": j})


def run_front(tok, gain, wq, wkv, gate, up, down, valid):
    sds = jax.ShapeDtypeStruct
    dma = pltpu.SemaphoreType.DMA
    return pl.pallas_call(
        front,
        out_shape=(
            sds((NMP, 2, TD, 128), BF),
            sds((NMP, 16, TD), BF),
            sds((8, 8, 2, 16, HB), BF),
            sds((8, 8, 2, 16, HB), BF),
            sds((64, D), BF),
            sds((TD, 1024), BF),
        ),
        in_specs=[VM, VM, ANY, ANY, VM, VM, VM, VM],
        out_specs=(ANY, ANY, ANY, ANY, VM, VM),
        scratch_shapes=[
            pltpu.VMEM((6, D, 512), BF),
            pltpu.VMEM((TD, D), BF),
            pltpu.VMEM((2, TD, 128), F32),
            pltpu.VMEM((NMP, 2, TD, 128), BF),
            pltpu.VMEM((16, TD), BF),
            pltpu.VMEM((8, 16, HB), BF),
            pltpu.VMEM((8, 16, HB), BF),
            pltpu.VMEM((TD, 512), F32),
            pltpu.VMEM((TD, 512), F32),
            dma((6,)), dma((NMP,)), dma((NMP,)), dma((NMP,)), dma((NMP,)),
            dma((8,)), dma((8,)), dma((8,)), dma((8,)), dma((4,)),
        ],
        compiler_params=pltpu.CompilerParams(
            collective_id=1, has_side_effects=True, vmem_limit_bytes=VLIM
        ),
        name="front",
    )(tok, gain, wq, wkv, gate, up, down, valid)


class Relay:
    def __init__(self, part, ssem, rsem):
        self.part, self.ssem, self.rsem = part, ssem, rsem
        dp, mp, chip, core = place()
        z, xh = lax.div(dp, 2), lax.rem(dp, 2)
        self.core, self.xh = core, xh
        self.zm, self.zp, self.z2, self.z = lax.rem(z + 3, 4), lax.rem(z + 1, 4), lax.rem(z + 2, 4), z
        self.xo = 1 - xh
        self.partner = {"mp": chip * 2 + 1 - core}
        self.up = {"dp": self.zp * 2 + xh}
        self.down = {"dp": self.zm * 2 + xh}
        self.across = {"dp": z * 2 + self.xo}
        self.count = 0
        self.started = []

    def put(self, block, parts, event, dev):
        for p in parts:
            ref = self.part(block, self.core, p)
            copy = send(ref, ref, self.ssem.at[self.count], self.rsem.at[event, p], dev)
            copy.start()
            self.started.append(copy)
            self.count += 1

    def got(self, block, parts, event, core=None):
        for p in parts:
            ref = self.part(block, self.core if core is None else core, p)
            landed(ref, self.ssem.at[0], self.rsem.at[event, p], self.partner)

    def finish(self):
        for copy in self.started:
            copy.wait_send()

    def stage0(self):
        b = self.z * 2 + self.xh
        self.put(b, (0, 1), 0, self.across)
        self.put(b, (0, 1), 1, self.up)
        self.put(b, (0, 1), 2, self.down)
        self.put(b, (0, 1), 8, self.partner)

    def stage1(self):
        b = self.z * 2 + self.xo
        self.got(b, (0, 1), 0)
        self.put(b, (0, 1), 3, self.up)
        self.put(b, (0, 1), 4, self.down)
        self.put(b, (0, 1), 9, self.partner)

    def stage2(self):
        b = self.zm * 2 + self.xh
        self.got(b, (0, 1), 1)
        self.put(b, (0,), 5, self.up)
        self.put(b, (0, 1), 10, self.partner)
        b = self.zp * 2 + self.xh
        self.got(b, (0, 1), 2)
        self.put(b, (1,), 5, self.down)
        self.put(b, (0, 1), 11, self.partner)

    def stage3(self):
        b = self.zm * 2 + self.xo
        self.got(b, (0, 1), 3)
        self.put(b, (0,), 6, self.up)
        self.put(b, (0, 1), 12, self.partner)
        b = self.zp * 2 + self.xo
        self.got(b, (0, 1), 4)
        self.put(b, (1,), 6, self.down)
        self.put(b, (0, 1), 13, self.partner)

    def stage4(self):
        b = self.z2 * 2 + self.xh
        self.got(b, (0, 1), 5)
        self.put(b, (0, 1), 14, self.partner)
        b = self.z2 * 2 + self.xo
        self.got(b, (0, 1), 6)
        self.put(b, (0, 1), 15, self.partner)

    def stage5(self):
        blocks = (
            self.z * 2 + self.xh, self.z * 2 + self.xo, self.zm * 2 + self.xh, self.zp * 2 + self.xh,
            self.zm * 2 + self.xo, self.zp * 2 + self.xo, self.z2 * 2 + self.xh, self.z2 * 2 + self.xo,
        )
        for e, b in enumerate(blocks):
            self.got(b, (0, 1), 8 + e, 1 - self.core)


def attend(
    qkv, flags, kvrows, lens, table, wg_i, wu_i,
    att_in, cache, wg, wu,
    qa, ka, va, fb, tile, pbuf, m_s, acc_s,
    ssem, rsem, asend, arecv, psend, precv, lsem,
):
    dp, mp, chip, core = place()
    others = [lax.rem(mp + s, NMP) for s in range(1, NMP)]
    dothers = [lax.rem(dp + s, NDP) for s in range(1, NDP)]
    barrier, count = greet([{"mp": j} for j in others] + [{"dp": i} for i in dothers])
    relay = Relay(lambda b, c, p: (wg, wu)[p].at[b, :, c], ssem, rsem)
    length = lens[0, 0]

    holder = [table[p, 0] for p in range(8)]
    target = []
    for p in range(8):
        rank = jnp.int32(0)
        for q in range(p):
            rank = rank + jnp.where(holder[q] == holder[p], 1, 0)
        target.append(holder[p] * 2 + rank)
    col = lax.broadcasted_iota(jnp.int32, (256, 128), 1)
    row = lax.broadcasted_iota(jnp.int32, (256, 128), 0)
    want = jnp.zeros((256, 128), jnp.int32)
    for p in range(8):
        want = jnp.where(lax.div(col, 16) == p, target[p], want)
    pick = (lax.div(row, 16) == want) & (lax.rem(row, 16) == lax.rem(col, 16))
    pick = jnp.where(pick, 1.0, 0.0).astype(BF)
    pages = jnp.dot(pick, kvrows[...], preferred_element_type=F32).astype(BF)
    for i in range(8):
        for r in range(2):
            pbuf[i, r] = pages[(i * 2 + r) * 16 : (i * 2 + r + 1) * 16]

    pl.semaphore_wait(barrier, count)
    relay.stage0()
    started = []
    own_pages = pltpu.make_async_copy(pbuf.at[dp], cache.at[dp], lsem.at[0])
    own_pages.start()
    for s in range(1, NDP):
        i = dothers[s - 1]
        copy = send(pbuf.at[i], cache.at[dp], psend.at[s], precv.at[s], {"dp": i})
        copy.start()
        started.append(copy)

    lane = lax.broadcasted_iota(jnp.int32, (TD, 128), 1)
    sub = lax.broadcasted_iota(jnp.int32, (TD, 128), 0)
    low = lane < 64

    def prepare(b, carry):
        q = qkv[b, 0].astype(F32)
        kv = qkv[b, 1].astype(F32)
        frow = flags[b].astype(F32)[0:1, :]
        token = sub + b * TD
        late = jnp.where(token >= length, 1.0, 0.0)
        extra = jnp.where(lane == 64, 1.0, jnp.where(lane == 65, late, 0.0))
        qi, half = lax.div(b, 2), lax.rem(b, 2)
        qa[qi, pl.ds(half * TD, TD), :] = jnp.where(low, q, extra).astype(BF)
        qa[qi, pl.ds(256 + half * TD, TD), :] = jnp.where(low, pltpu.roll(q, 64, 1), extra).astype(BF)
        fcol = jnp.sum(jnp.where(lane == sub, frow, 0.0), axis=1, keepdims=True)
        closed = jnp.where(fcol > 0.5, 0.0, NEG)
        early = jnp.where(token >= length, 0.0, NEG)
        bias = jnp.where(lane == 64, closed, jnp.where(lane == 65, early, 0.0))
        ka[qi, pl.ds(half * TD, TD), :] = jnp.where(low, kv, bias).astype(BF)
        one = jnp.where(lane == 64, 1.0, 0.0)
        va[qi, pl.ds(half * TD, TD), :] = jnp.where(low, pltpu.roll(kv, 64, 1), one).astype(BF)
        fb[b] = jnp.broadcast_to(frow, (8, TD))
        return carry

    lax.fori_loop(0, NMP, prepare, 0)

    trow = lax.broadcasted_iota(jnp.int32, (512, 256), 0)
    trow = lax.rem(trow, 256)
    tcol = lax.broadcasted_iota(jnp.int32, (512, 256), 1)
    nt = (((1,), (1,)), ((), ()))
    qlane = lax.broadcasted_iota(jnp.int32, (512, 128), 1)
    hlane = lax.broadcasted_iota(jnp.int32, (256, 128), 1)

    def block(qi, carry):
        q = qa[qi]
        bare = jnp.where(qlane < 64, q.astype(F32), 0.0).astype(BF)
        s = lax.dot_general(bare, ka[qi], nt, preferred_element_type=F32)
        open_row = jnp.concatenate([fb[2 * qi][0:1], fb[2 * qi + 1][0:1]], axis=1) > 0.5
        base = qi * 256
        split = (trow + base >= length) & (tcol + base < length)
        ok = ((tcol < trow) & open_row & jnp.logical_not(split)) | (tcol == trow)
        s = jnp.where(ok, s, NEG)
        m = jnp.max(s, axis=1, keepdims=True)
        p = jnp.exp2(s - m)
        acc = jnp.dot(p.astype(BF), va[qi], preferred_element_type=F32)
        m_s[...] = m
        acc_s[...] = acc

        def step(ki, c2):
            s = lax.dot_general(qa[qi], ka[ki], nt, preferred_element_type=F32)
            m = m_s[...]
            m_new = jnp.maximum(m, jnp.max(s, axis=1, keepdims=True))
            p = jnp.exp2(s - m_new)
            acc_s[...] = acc_s[...] * jnp.exp2(m - m_new) + jnp.dot(
                p.astype(BF), va[ki], preferred_element_type=F32
            )
            m_s[...] = m_new
            return c2

        lax.fori_loop(0, qi, step, 0)
        acc = acc_s[...]
        out = acc / acc[:, 64:65]
        both = jnp.where(hlane < 64, out[:256], pltpu.roll(out[256:], 64, 1)).astype(BF)
        for half in range(2):
            j = 2 * qi + half
            tile[j] = both[half * TD : (half + 1) * TD]

            @pl.when(j != mp)
            def _():
                send(tile.at[j], att_in.at[mp], asend.at[j], arecv.at[mp], {"mp": j}).start()

            @pl.when(j == mp)
            def _():
                pltpu.make_async_copy(tile.at[j], att_in.at[j], lsem.at[1]).start()

        return carry

    lax.fori_loop(0, 4, block, 0)
    relay.stage2()
    lax.fori_loop(4, 5, block, 0)
    relay.stage1()
    lax.fori_loop(5, 7, block, 0)
    relay.stage3()
    lax.fori_loop(7, 8, block, 0)
    relay.stage4()
    relay.stage5()
    pltpu.make_async_copy(tile.at[mp], att_in.at[mp], lsem.at[1]).wait()
    for s in range(1, NMP):
        j = others[s - 1]
        copy = send(tile.at[j], att_in.at[j], asend.at[j], arecv.at[j], {"mp": j})
        copy.wait_send()
        copy.wait_recv()
    own_pages.wait()
    for s in range(1, NDP):
        started[s - 1].wait_send()
        i = lax.rem(dp + NDP - s, NDP)
        landed(cache.at[i], psend.at[s], precv.at[s], {"dp": i})
    relay.finish()


def run_attend(qkv, flags, kvrows, lens, table, wg, wu):
    sds = jax.ShapeDtypeStruct
    dma = pltpu.SemaphoreType.DMA
    return pl.pallas_call(
        attend,
        out_shape=(
            sds((NMP, TD, 128), BF),
            sds((NDP, 2, 16, 1024), BF),
            sds(wg.shape, BF),
            sds(wu.shape, BF),
        ),
        in_specs=[VM, VM, VM, SM, SM, ANY, ANY],
        out_specs=(ANY, ANY, ANY, ANY),
        input_output_aliases={5: 2, 6: 3},
        scratch_shapes=[
            pltpu.VMEM((8, 512, 128), BF),
            pltpu.VMEM((8, 256, 128), BF),
            pltpu.VMEM((8, 256, 128), BF),
            pltpu.VMEM((NMP, 8, TD), F32),
            pltpu.VMEM((NMP, TD, 128), BF),
            pltpu.VMEM((NDP, 2, 16, 1024), BF),
            pltpu.VMEM((512, 1), F32),
            pltpu.VMEM((512, 128), F32),
            dma((30,)), dma((16, 2)), dma((NMP,)), dma((NMP,)), dma((NDP,)), dma((NDP,)), dma((2,)),
        ],
        compiler_params=pltpu.CompilerParams(
            collective_id=2, has_side_effects=True, vmem_limit_bytes=VLIM
        ),
        name="attend",
    )(qkv, flags, kvrows, lens, table, wg, wu)


def mlp(
    att, tok, gain, wo, wg, wu, wd,
    out,
    att_v, wo_v, wg_v, wu_v, wd_v, hid, act, hbuf, part, rs, via,
    wsem, gs, gr, ss, sr, wss, wsr,
):
    dp, mp, chip, core = place()
    y, x = lax.div(chip, 2), lax.rem(chip, 2)
    yp, ym, y2, xo = lax.rem(y + 1, 4), lax.rem(y + 3, 4), lax.rem(y + 2, 4), 1 - x

    def dev(yy, xx):
        return {"mp": (yy * 2 + xx) * 2 + core}

    peers = [(y, xo), (yp, x), (ym, x), (yp, xo), (ym, xo), (y2, x), (y2, xo)]
    relay = Relay(lambda b, c, p: wd_v.at[b, c, pl.ds(p * 32, 32)], wss, wsr)
    barrier, count = greet([dev(*p) for p in peers] + [relay.partner, relay.up, relay.down, relay.across])
    loads = [
        pltpu.make_async_copy(wg, wg_v, wsem.at[0]),
        pltpu.make_async_copy(wu, wu_v, wsem.at[1]),
        pltpu.make_async_copy(wd, wd_v.at[dp, core], wsem.at[2]),
    ]
    wo_loads = [
        pltpu.make_async_copy(wo.at[:, pl.ds(n * 512, 512)], wo_v.at[n], wsem.at[3 + n]) for n in range(4)
    ]
    loads[2].start()
    for copy in wo_loads:
        copy.start()
    pl.semaphore_wait(barrier, count)
    loads[2].wait()
    relay.stage0()
    for j in range(NMP):
        att_v[:, j * 128 : (j + 1) * 128] = att[j]
    for n in range(4):
        cols = slice(n * 512, (n + 1) * 512)
        wo_loads[n].wait()
        got = jnp.dot(att_v[...], wo_v[n], preferred_element_type=F32)
        hid[:, cols] = (tok[:, cols].astype(F32) + got).astype(BF).astype(F32)
    for copy in loads[:2]:
        copy.start()
    act[chip] = norm_rows(hid[...], gain[...]).astype(BF)

    started = []
    half = (pl.ds(0, 64), pl.ds(64, 64))
    inner = (pl.ds(64 - INNER, INNER), pl.ds(64, INNER))
    both = pl.ds(64 - INNER, 2 * INNER)
    outer = (pl.ds(0, 64 - INNER), pl.ds(64 + INNER, 64 - INNER))

    def forward(block, rows, event, to):
        ref = act.at[block] if rows is None else act.at[block, rows]
        copy = send(ref, ref, gs.at[len(started)], gr.at[event], dev(*to))
        copy.start()
        started.append(copy)

    def arrive(block, rows, event):
        ref = act.at[block] if rows is None else act.at[block, rows]
        landed(ref, gs.at[0], gr.at[event], dev(y, xo))

    def slot(yy, xx):
        return yy * 2 + xx

    mine = slot(y, x)
    forward(mine, None, 0, (y, xo))
    forward(mine, None, 1, (yp, x))
    forward(mine, None, 2, (ym, x))
    relay.stage2()
    relay.stage1()
    arrive(slot(y, xo), None, 0)
    for i in range(2):
        forward(slot(y, xo), outer[i], 3 + i, (yp, x))
        forward(slot(y, xo), outer[i], 5 + i, (ym, x))
    arrive(slot(ym, x), None, 1)
    forward(slot(ym, x), half[0], 7, (yp, x))
    forward(slot(ym, x), both, 9, (y, xo))
    arrive(slot(yp, x), None, 2)
    forward(slot(yp, x), half[1], 8, (ym, x))
    forward(slot(yp, x), both, 10, (y, xo))
    relay.stage3()
    for copy in loads[:2]:
        copy.wait()

    def widen(k, yy):
        rows = act.at[pl.ds(yy * 2, 2)]

        def hidden(n, carry):
            cols = pl.ds(pl.multiple_of(n * 256, 256), 256)
            xin = rows[...].reshape(256, D)
            g = jnp.dot(xin, wg_v[:, cols], preferred_element_type=F32)
            u = jnp.dot(xin, wu_v[:, cols], preferred_element_type=F32)
            hbuf[k, :, cols] = (g / (1.0 + jnp.exp(-g)) * u).astype(BF)
            return carry

        lax.fori_loop(0, 4, hidden, 0)

    def narrow(k, yy, start=0, stop=4):
        def final(n, carry):
            cols = pl.ds(pl.multiple_of(n * 512, 512), 512)
            w = wd_v[:, :, :, cols].reshape(HB, 512)
            r = jnp.dot(hbuf[k], w, preferred_element_type=F32).astype(BF)
            part[yy * 2, :, cols] = r[:TD]
            part[yy * 2 + 1, :, cols] = r[TD:]
            return carry

        lax.fori_loop(start, stop, final, 0)

    sends = []

    def ship(src, dst, event, to):
        copy = send(src, dst, ss.at[event], sr.at[event], dev(*to))
        copy.start()
        sends.append(copy)

    def give(yy, xx, rows, event):
        ship(part.at[slot(yy, xx), rows], rs.at[mine, rows], event, (yy, xx))

    def taken(dst, event):
        landed(dst, ss.at[event], sr.at[event], dev(y, xo))

    widen(0, y)
    arrive(slot(ym, xo), outer[0], 3)
    forward(slot(ym, xo), outer[0], 11, (yp, x))
    arrive(slot(yp, xo), outer[1], 6)
    forward(slot(yp, xo), outer[1], 12, (ym, x))
    relay.stage4()
    arrive(slot(ym, xo), outer[1], 4)
    arrive(slot(ym, xo), both, 9)
    widen(1, ym)
    arrive(slot(y2, x), half[0], 7)
    forward(slot(y2, x), inner[0], 13, (y, xo))
    arrive(slot(y2, x), half[1], 8)
    forward(slot(y2, x), inner[1], 14, (y, xo))
    arrive(slot(yp, xo), outer[0], 5)
    arrive(slot(yp, xo), both, 10)
    widen(2, yp)
    relay.stage5()
    narrow(1, ym)
    for k, xx in enumerate((x, xo)):
        give(ym, xx, half[0], 1 + k)
    narrow(2, yp)
    for k, xx in enumerate((x, xo)):
        give(yp, xx, half[1], 3 + k)
    for i in range(2):
        arrive(slot(y2, xo), outer[i], 11 + i)
        arrive(slot(y2, xo), inner[i], 13 + i)
    widen(3, y2)
    wide = (pl.ds(0, 1024), pl.ds(1024, 1024))
    for c in range(2):
        narrow(3, y2, 2 * c, 2 * c + 2)
        for k, xx in enumerate((xo, x)):
            ship(part.at[slot(y2, xx), half[0], wide[c]], via.at[0, k, :, wide[c]], 5 + 8 * c + k, (yp, x))
            ship(part.at[slot(y2, xx), half[1], wide[c]], via.at[1, k, :, wide[c]], 7 + 8 * c + k, (ym, x))
    narrow(0, y)
    give(y, xo, pl.ds(0, TD), 0)
    for c in range(2):
        for k, xx in enumerate((xo, x)):
            for side, (yy, event) in enumerate(((yp, 9), (ym, 11))):
                got = via.at[side, k, :, wide[c]]
                taken(got, 5 + 8 * c + 2 * side + k)
                ref = part.at[slot(yy, xx), half[side], wide[c]]
                ref[...] = (ref[...].astype(F32) + got[...].astype(F32)).astype(BF)
                ship(ref, rs.at[mine, half[side], wide[c]], event + 8 * c + k, (yy, xx))
    taken(rs.at[slot(y, xo)], 0)
    for k, xx in enumerate((x, xo)):
        taken(rs.at[slot(yp, xx), half[0]], 1 + k)
        taken(rs.at[slot(ym, xx), half[1]], 3 + k)
    for c in range(2):
        for k, xx in enumerate((xo, x)):
            taken(rs.at[slot(ym, xx), half[0], wide[c]], 9 + 8 * c + k)
            taken(rs.at[slot(yp, xx), half[1], wide[c]], 11 + 8 * c + k)
    sources = [slot(y, xo), slot(ym, x), slot(ym, xo), slot(yp, x), slot(yp, xo)]

    def close(n, carry):
        cols = pl.ds(pl.multiple_of(n * 256, 256), 256)
        total = part[mine, :, cols].astype(F32)
        for c in sources:
            total = total + rs[c, :, cols].astype(F32)
        out[:, cols] = (hid[:, cols] + total).astype(BF)
        return carry

    lax.fori_loop(0, 8, close, 0)
    for copy in started + sends:
        copy.wait_send()
    relay.finish()


def run_mlp(att, tok, gain, wo, wg, wu, wd):
    dma = pltpu.SemaphoreType.DMA
    return pl.pallas_call(
        mlp,
        out_shape=jax.ShapeDtypeStruct((TD, D), BF),
        in_specs=[VM, VM, VM, ANY, ANY, ANY, ANY],
        out_specs=VM,
        scratch_shapes=[
            pltpu.VMEM((TD, D), BF),
            pltpu.VMEM((4, D, 512), BF),
            pltpu.VMEM((D, HB), BF),
            pltpu.VMEM((D, HB), BF),
            pltpu.VMEM((8, 2, 64, D), BF),
            pltpu.VMEM((TD, D), F32),
            pltpu.VMEM((8, TD, D), BF),
            pltpu.VMEM((4, 256, HB), BF),
            pltpu.VMEM((8, TD, D), BF),
            pltpu.VMEM((8, TD, D), BF),
            pltpu.VMEM((2, 2, 64, D), BF),
            dma((7,)), dma((15,)), dma((15,)), dma((21,)), dma((21,)), dma((30,)), dma((16, 2)),
        ],
        compiler_params=pltpu.CompilerParams(
            collective_id=3, has_side_effects=True, vmem_limit_bytes=VLIM
        ),
        name="mlp",
    )(att, tok, gain, wo, wg, wu, wd)


def on_device(
    tokens, attn_gain, mlp_gain, query_weight, keyval_weight, output_weight,
    gate_rows, up_rows, down_rows, lengths, valid, page_table,
):
    qkv, flags, wg, wu, wd, kvrows = run_front(
        tokens, attn_gain.reshape(1, D), query_weight, keyval_weight,
        gate_rows, up_rows, down_rows, valid.reshape(1, TD),
    )
    att, cache, wg, wu = run_attend(qkv, flags, kvrows, lengths, page_table, wg, wu)
    layer_out = run_mlp(
        att, tokens, mlp_gain.reshape(1, D), output_weight,
        wg.reshape(D, HB), wu.reshape(D, HB), wd,
    )
    return (layer_out, cache[None, None])


def solution(mesh):
    return jax.shard_map(
        on_device,
        mesh=mesh,
        in_specs=(
            P(("dp", "mp"), None), P(), P(), P(), P(), P(),
            P(("dp", "mp"), None), P(("dp", "mp"), None), P(("dp", "mp"), None),
            P("dp", None), P(("dp", "mp")), P(("dp", "mp"), None),
        ),
        out_specs=(P(("dp", "mp"), None), P("dp", "mp", None, None, None, None)),
        check_vma=False,
    )
```
